512 devices in a mesh: dp: 8 (over y, core), expert: 64 (over x, z).
Axes of the slice: x: 4, y: 4, z: 16, core: 2. Of those that a mesh axis runs over, the one named last changes fastest.
Arguments:
- tokens: bfloat16 [65536, 4096], P(('dp', 'expert')), may hold values from -6 to 6
- expert_ids: int32 [65536, 2], P(('dp', 'expert')), may hold values from 0 to 63, as said below
- gate_values: float32 [65536, 2], P(('dp', 'expert')), may hold values from 0.2 to 1
- w_gate: bfloat16 [4096, 14336], P('dp', 'expert'), may hold values from -0.09375 to 0.09375
- w_up: bfloat16 [4096, 14336], P('dp', 'expert'), may hold values from -0.09375 to 0.09375
- w_down: bfloat16 [14336, 4096], P('expert', 'dp'), may hold values from -0.046875 to 0.046875
- target: bfloat16 [65536, 4096], P(('dp', 'expert')), may hold values from -6 to 6
Outputs:
- token_grad: bfloat16 [65536, 4096], P(('dp', 'expert'))
- gate_grad: bfloat16 [4096, 14336], P('dp', 'expert')
- up_grad: bfloat16 [4096, 14336], P('dp', 'expert')
The draws below stay inside these ranges and needn't reach their ends.
Inputs may be any that keep to these rules, and one draw needn't show every extreme that they name: `expert_ids`: A token's two expert ids differ, and no token names two experts below 1. Among the 128 tokens of one device each expert below 1 is named by 1 to 3 tokens, and in every draw some device names each of them exactly 3 times.
All inputs are finite; a program needn't handle non-finite values.
Results may differ from the reference program's by a relative error of at most 0.008.
Values may be sent and summed in bfloat16 or wider, within the bound.
A program may use at most 64 MiB of HBM per device.

```python
import math
import jax
import jax.numpy as jnp
from jax import lax

D = 4096
HID = 14336
ROUTED = 64
EXPERTS = 1
TOK_DEV = 128
GROUP = 64
CAP = 3
TOKENS = 65536
N_DP = 8
N_EXPERT = 64


def draw_expert_ids(key, part):
    blocks = N_DP * N_EXPERT
    key_counts, key_full, key_perm, key_first, key_second, key_order = jax.random.split(key, 6)
    counts = jax.random.randint(key_counts, (blocks, EXPERTS), 1, CAP + 1)
    full_block = jax.random.randint(key_full, (), 0, blocks)
    counts = jnp.where(jnp.arange(blocks)[:, None] == full_block, CAP, counts)
    count_ends = jnp.cumsum(counts, axis=1)
    permuted = jax.vmap(lambda one_key: jax.random.permutation(one_key, TOK_DEV))(jax.random.split(key_perm, blocks))
    token_rank = jnp.argsort(permuted, axis=1)
    window_expert = jnp.sum((token_rank[:, :, None] >= count_ends[:, None, :]).astype(jnp.int32), axis=2)
    in_window = window_expert < EXPERTS
    outside = ROUTED - EXPERTS
    first_choice = EXPERTS + jax.random.randint(key_first, (blocks, TOK_DEV), 0, outside)
    second = EXPERTS + (first_choice - EXPERTS + jax.random.randint(key_second, (blocks, TOK_DEV), 1, outside)) % outside
    chosen = jnp.where(in_window, window_expert, second)
    swap_order = jax.random.randint(key_order, (blocks, TOK_DEV), 0, 2)
    column_zero = jnp.where(swap_order == 1, chosen, first_choice)
    column_one = jnp.where(swap_order == 1, first_choice, chosen)
    return jnp.stack([column_zero, column_one], axis=-1).reshape(blocks * TOK_DEV, 2).astype(jnp.int32)


def block_scale(key, dims, cuts, smallest, high):
    level = 1.0
    for dim, shards_of in cuts:
        draws = jax.random.uniform(jax.random.fold_in(jax.random.fold_in(key, 6), dim), (shards_of,), jnp.float32, smallest / len(cuts), high / len(cuts))
        level = level * jnp.repeat(jnp.exp(draws), dims[dim] // shards_of).reshape((-1,) + (1,) * (len(dims) - 1 - dim))
    return level


def centred(own_key, extent, spread, limit, cuts=(), kind=jnp.bfloat16):
    drawn = jax.random.normal(own_key, extent, jnp.float32) * spread
    if len(cuts) > 0:
        drawn = block_scale(own_key, extent, cuts, -0.22, 0.18) * drawn
    return jnp.clip(drawn, min=-limit, max=limit).astype(kind)


def setup_inputs(seed: int = 0) -> dict:
    seeds = jax.random.split(jax.random.key(seed), 8)
    tokens = centred(seeds[0], (TOKENS, D), 1.0, 6.0, ((0, 512),))
    expert_ids = draw_expert_ids(jax.random.fold_in(seeds[7], 71), 0)
    gate_values = jnp.clip(jnp.exp(math.log(1.0) - 1.609438 * jax.random.uniform(seeds[2], (TOKENS, 2), jnp.float32) ** block_scale(seeds[2], (TOKENS, 2), ((0, 512),), -0.2, 0.2)), 0.2, 1.0)
    w_gate = centred(seeds[3], (D, EXPERTS * HID), D ** -0.5, 0.09375, ((0, 8), (1, 64)))
    w_up = centred(seeds[4], (D, EXPERTS * HID), D ** -0.5, 0.09375, ((0, 8), (1, 64)))
    w_down = centred(seeds[5], (EXPERTS * HID, D), HID ** -0.5, 0.046875, ((0, 64), (1, 8)))
    target = centred(seeds[6], (TOKENS, D), 1.0, 6.0, ((0, 512),))
    return dict(tokens=tokens, expert_ids=expert_ids, gate_values=gate_values, w_gate=w_gate, w_up=w_up, w_down=w_down, target=target)


def slot_tables(expert_ids, gate_values):
    blocks = N_DP * N_EXPERT
    pair_count = 2 * TOK_DEV
    route_ids = expert_ids.reshape(blocks, pair_count).astype(jnp.int32)
    onehot = (route_ids[:, :, None] == jnp.arange(EXPERTS, dtype=jnp.int32)[None, None, :]).astype(jnp.int32)
    slot_index = jnp.sum((jnp.cumsum(onehot, axis=1) - onehot) * onehot, axis=2).astype(jnp.int32)
    window = route_ids < EXPERTS
    position = jnp.where(window, route_ids * CAP + slot_index, EXPERTS * CAP).astype(jnp.int32)
    block_index = jnp.arange(blocks, dtype=jnp.int32)[:, None]
    owning = (block_index * TOK_DEV + jnp.arange(pair_count, dtype=jnp.int32)[None, :] // 2).astype(jnp.int32)
    table_width = EXPERTS * CAP + 1
    slot_token = jnp.zeros((blocks, table_width), jnp.int32).at[block_index, position].set(owning)[:, :-1]
    slot_live = jnp.zeros((blocks, table_width), jnp.float32).at[block_index, position].set(1.0)[:, :-1]
    slot_gate = jnp.zeros((blocks, table_width), jnp.float32).at[block_index, position].set(
        gate_values.astype(jnp.float32).reshape(blocks, pair_count))[:, :-1]
    return route_ids, window, position, slot_token, slot_live, slot_gate


def by_receiver(table):
    shaped = table.reshape(N_DP, N_EXPERT, EXPERTS, CAP)
    return jnp.transpose(shaped, (0, 2, 1, 3)).reshape(N_DP, EXPERTS, N_EXPERT * CAP)


def reference(tokens, expert_ids, gate_values, w_gate, w_up, w_down, target):
    route_ids, window, position, slot_token, slot_live, slot_gate = slot_tables(expert_ids, gate_values)
    recv_token = by_receiver(slot_token)
    recv_live = by_receiver(slot_live)
    recv_gate = by_receiver(slot_gate)
    rows_count = N_EXPERT * CAP
    hid_local = HID // GROUP

    def rows_for(dp_index, expert_index):
        token_index = recv_token[dp_index, expert_index]
        live_mask = recv_live[dp_index, expert_index]
        return jnp.where(live_mask[:, None] > 0, tokens[token_index], jnp.zeros((), tokens.dtype))

    def slices(expert_index, slice_index):
        column_start = (expert_index * HID + slice_index * hid_local).astype(jnp.int32)
        gate_slice = lax.dynamic_slice_in_dim(w_gate, column_start, hid_local, 1)
        up_slice = lax.dynamic_slice_in_dim(w_up, column_start, hid_local, 1)
        down_slice = lax.dynamic_slice_in_dim(w_down, column_start, hid_local, 0)
        return gate_slice, up_slice, down_slice

    def forward_item(item_index):
        dp_index = item_index // EXPERTS
        expert_index = item_index % EXPERTS
        rows_in = rows_for(dp_index, expert_index)

        def slice_step(running, slice_index):
            gate_slice, up_slice, down_slice = slices(expert_index, slice_index)
            gate_pre = jnp.dot(rows_in, gate_slice, preferred_element_type=jnp.float32)
            up_pre = jnp.dot(rows_in, up_slice, preferred_element_type=jnp.float32)
            hidden = (jax.nn.sigmoid(gate_pre) * gate_pre * up_pre).astype(jnp.bfloat16)
            partial_value = jnp.dot(hidden, down_slice, preferred_element_type=jnp.float32).astype(jnp.bfloat16)
            return running + partial_value.astype(jnp.float32), None

        running, _ = lax.scan(slice_step, jnp.zeros((rows_count, D), jnp.float32), jnp.arange(GROUP, dtype=jnp.int32))
        return running

    outputs_all = lax.map(forward_item, jnp.arange(N_DP * EXPERTS, dtype=jnp.int32))
    blocks = N_DP * N_EXPERT
    block_index = jnp.arange(blocks, dtype=jnp.int32)[:, None]
    dp_of = block_index // N_EXPERT
    source = block_index % N_EXPERT
    safe_ids = jnp.where(window, route_ids, 0).astype(jnp.int32)
    slot_part = (jnp.where(window, position, 0) % CAP).astype(jnp.int32)
    fwd_rows = ((dp_of * EXPERTS + safe_ids) * rows_count + source * CAP + slot_part).reshape(TOKENS, 2).astype(jnp.int32)
    bwd_rows = ((safe_ids * N_DP + dp_of) * rows_count + source * CAP + slot_part).reshape(TOKENS, 2).astype(jnp.int32)
    live_pair = window.reshape(TOKENS, 2)
    flat_out = outputs_all.reshape(-1, D)
    gate_f = gate_values.astype(jnp.float32)
    first_pick = jnp.where(live_pair[:, 0:1], flat_out[fwd_rows[:, 0]], 0.0)
    second_pick = jnp.where(live_pair[:, 1:2], flat_out[fwd_rows[:, 1]], 0.0)
    combined = gate_f[:, 0:1] * first_pick + gate_f[:, 1:2] * second_pick
    residual = combined - target.astype(jnp.float32)

    def backward_expert(expert_index):
        def dp_step(accumulated, dp_index):
            gate_acc, up_acc = accumulated
            rows_in = rows_for(dp_index, expert_index)
            token_index = recv_token[dp_index, expert_index]
            live_mask = recv_live[dp_index, expert_index]
            gate_row = recv_gate[dp_index, expert_index]
            cotangent = jnp.where(live_mask[:, None] > 0, gate_row[:, None] * residual[token_index], 0.0).astype(jnp.bfloat16)

            def slice_step(carry, slice_index):
                row_acc, gate_inner, up_inner = carry
                gate_slice, up_slice, down_slice = slices(expert_index, slice_index)
                gate_pre = jnp.dot(rows_in, gate_slice, preferred_element_type=jnp.float32)
                up_pre = jnp.dot(rows_in, up_slice, preferred_element_type=jnp.float32)
                sigmoid_gate = jax.nn.sigmoid(gate_pre)
                activated = sigmoid_gate * gate_pre
                grad_hidden = jnp.dot(cotangent, down_slice.T, preferred_element_type=jnp.float32)
                derivative = sigmoid_gate * (1.0 + gate_pre * (1.0 - sigmoid_gate))
                grad_gate_pre = (grad_hidden * up_pre * derivative).astype(jnp.bfloat16)
                grad_up_pre = (grad_hidden * activated).astype(jnp.bfloat16)
                row_part = (jnp.dot(grad_gate_pre, gate_slice.T, preferred_element_type=jnp.float32)
                            + jnp.dot(grad_up_pre, up_slice.T, preferred_element_type=jnp.float32)).astype(jnp.bfloat16)
                gate_term = lax.optimization_barrier(jnp.dot(rows_in.T, grad_gate_pre, preferred_element_type=jnp.float32).astype(jnp.bfloat16))
                up_term = lax.optimization_barrier(jnp.dot(rows_in.T, grad_up_pre, preferred_element_type=jnp.float32).astype(jnp.bfloat16))
                column = (slice_index * hid_local).astype(jnp.int32)
                gate_inner = lax.dynamic_update_slice_in_dim(
                    gate_inner, lax.dynamic_slice_in_dim(gate_inner, column, hid_local, 1) + gate_term.astype(jnp.float32), column, 1)
                up_inner = lax.dynamic_update_slice_in_dim(
                    up_inner, lax.dynamic_slice_in_dim(up_inner, column, hid_local, 1) + up_term.astype(jnp.float32), column, 1)
                return (row_acc + row_part.astype(jnp.float32), gate_inner, up_inner), None

            start_rows = jnp.zeros((rows_count, D), jnp.float32)
            (row_acc, gate_acc, up_acc), _ = lax.scan(slice_step, (start_rows, gate_acc, up_acc), jnp.arange(GROUP, dtype=jnp.int32))
            return (gate_acc, up_acc), row_acc

        start_grads = (jnp.zeros((D, HID), jnp.float32), jnp.zeros((D, HID), jnp.float32))
        (gate_acc, up_acc), row_sums = lax.scan(dp_step, start_grads, jnp.arange(N_DP, dtype=jnp.int32))
        return gate_acc, up_acc, row_sums

    gate_all, up_all, row_all = lax.map(backward_expert, jnp.arange(EXPERTS, dtype=jnp.int32))
    flat_rows = row_all.reshape(-1, D)
    first_grad = jnp.where(live_pair[:, 0:1], flat_rows[bwd_rows[:, 0]], 0.0)
    second_grad = jnp.where(live_pair[:, 1:2], flat_rows[bwd_rows[:, 1]], 0.0)
    token_grad = (first_grad + second_grad).astype(jnp.bfloat16)
    gate_grad = jnp.transpose(gate_all, (1, 0, 2)).reshape(D, EXPERTS * HID).astype(jnp.bfloat16)
    up_grad = jnp.transpose(up_all, (1, 0, 2)).reshape(D, EXPERTS * HID).astype(jnp.bfloat16)
    return (token_grad, gate_grad, up_grad)
```

```python
import functools

import jax
import jax.numpy as jnp
from jax import lax
from jax.experimental import pallas as pl
from jax.experimental.pallas import tpu as pltpu
from jax.sharding import PartitionSpec as P

MESH = pl.DeviceIdType.MESH
F32, BF16 = jnp.float32, jnp.bfloat16
CAP = 3
NX = 4
NL = 4


def dot_nn(a, b):
    return jnp.dot(a, b, preferred_element_type=F32)


def dot_nt(a, b):
    return lax.dot_general(a, b, (((1,), (1,)), ((), ())), preferred_element_type=F32)


def dot_tn(a, b):
    return lax.dot_general(a, b, (((0,), (0,)), ((), ())), preferred_element_type=F32)


def ds(start, size, unit):
    return pl.ds(pl.multiple_of(start, unit), size)


def layer_kernel(
    nx, nz, ndp, tok_ref, tgt_ref, ids_ref, gv_ref, wg_ref, wu_ref, wd_ref,
    tg_out, gg_out, ug_out,
    wg, wu, wd, fx, fc, p1, p2, xc, gga,
    msg, rmsg, msg2, rmsg2, xs, ts, gs, rg, rows, sel,
    gacc, uacc, hid, ga, ua,
    rx0, rl1, rl0, rx1, rh, s0, s1, tt,
    sems,
):
    nh, ny = nz // NL, ndp // 2
    tok_rows, width = tok_ref.shape
    slots, rall = nz * CAP, nx * nz * CAP
    half = width // 2
    cw = half // nz
    clw = nh * cw
    dsh = width // ndp
    hloc = wg_ref.shape[0]
    hp = gga.shape[2] // 2

    dp, e = lax.axis_index("dp"), lax.axis_index("expert")
    y, c = dp // 2, dp % 2
    x, z = e // nz, e % nz
    r, zh = z % NL, z // NL
    blk = r * nh + zh

    def at_z(k):
        return (dp, x * nz + (z + k + nz) % nz)

    def at_x(k):
        return (dp, (x + k) % nx * nz + z)

    def at_dp(i):
        return (i, e)

    partner = at_dp(y * 2 + 1 - c)
    xrows = ds(x * slots, slots, 16)
    used = [0]

    def send(src, dst, dev):
        n = used[0]
        used[0] += 1
        cp = pltpu.make_async_remote_copy(
            src_ref=src, dst_ref=dst, send_sem=sems.at[0, n], recv_sem=sems.at[1, n],
            device_id=dev, device_id_type=MESH,
        )
        cp.start()
        return cp

    barrier = pltpu.get_barrier_semaphore()
    peers = [at_z(k) for k in range(1, nz)] + [at_x(k) for k in range(1, nx)]
    peers += [at_dp((dp + k) % ndp) for k in range(1, ndp)]
    for dev in peers:
        pl.semaphore_signal(barrier, inc=1, device_id=dev, device_id_type=MESH)
    pl.semaphore_wait(barrier, len(peers))

    def shard_of(i):
        return ds(i * dsh, dsh, 128)

    wsends, wcore = [], []
    for shard, full in ((wg_ref, wg), (wu_ref, wu), (wd_ref, wd)):
        mine = full.at[:, shard_of(dp)]
        wsends.append([send(shard, mine, at_dp((y + k) % ny * 2 + c)) for k in range(1, ny)])
        wcore.append(send(shard, mine, partner))
    for shard, full in ((wg_ref, wg), (wu_ref, wu), (wd_ref, wd)):
        full[:, shard_of(dp)] = shard[...]

    computed0 = ids_ref[0:1, :] < 1
    computed = jnp.logical_or(computed0, ids_ref[1:2, :] < 1)
    live = jnp.where(computed, 1.0, 0.0).astype(F32)
    gate = jnp.where(computed0, gv_ref[0:1, :], gv_ref[1:2, :])
    before = lax.broadcasted_iota(jnp.int32, (tok_rows, tok_rows), 0) < lax.broadcasted_iota(
        jnp.int32, (tok_rows, tok_rows), 1
    )
    live8 = jnp.broadcast_to(live, (8, tok_rows))
    slot = dot_nn(live8.astype(BF16), jnp.where(before, 1.0, 0.0).astype(BF16))
    row8 = lax.broadcasted_iota(jnp.int32, (8, tok_rows), 0).astype(F32)
    selx = jnp.where(slot == row8, live8, 0.0)
    selt = jnp.where(slot == row8 - 3.0, live8, 0.0)
    sel[...] = selx
    gsel = jnp.where(live8 > 0, selx * gate, 0.0)
    g0 = jnp.sum(gsel[0:1], axis=1, keepdims=True)
    g1 = jnp.sum(gsel[1:2], axis=1, keepdims=True)
    g2 = jnp.sum(gsel[2:3], axis=1, keepdims=True)
    rowc = lax.broadcasted_iota(jnp.int32, (8, cw), 0)
    gleft = jnp.where(rowc == 6, g0, jnp.where(rowc == 7, g2, 0.0))
    gright = jnp.where(rowc == 6, g1, 0.0)
    selx, selt = selx.astype(BF16), selt.astype(BF16)
    for k in range(nz):
        col = ((k % NL) * nh + k // NL) * cw
        for h, extra in ((0, gleft), (1, gright)):
            cols = slice(h * half + col, h * half + col + cw)
            piece = dot_nn(selx, tok_ref[:, cols]) + dot_nn(selt, tgt_ref[:, cols])
            msg[k, :, h * cw : (h + 1) * cw] = piece + extra
    rmsg[pl.ds(z, 1)] = msg[pl.ds(z, 1)]
    cps = [send(msg.at[(z + k) % nz], rmsg.at[z], at_z(k)) for k in range(1, nz)]
    for cp in cps:
        cp.wait()
    for k in range(nz):
        b = CAP * k
        xs[b : b + 3, :] = rmsg[k, 0:3, :]
        ts[b : b + 3, :] = rmsg[k, 3:6, :]
        gs[b : b + 1, :] = rmsg[k, 6:7, 0:cw]
        gs[b + 1 : b + 2, :] = rmsg[k, 6:7, cw : 2 * cw]
        gs[b + 2 : b + 3, :] = rmsg[k, 7:8, 0:cw]

    def along_l(ref_of):
        out = []
        for idx, k in enumerate((1, -1)):
            src, dst = ref_of(k, idx, 0, clw)
            out.append(send(src, dst, at_z(k)))
        for k, lo in ((2, 0), (-2, clw // 2)):
            src, dst = ref_of(k, 2, lo, clw // 2)
            out.append(send(src, dst, at_z(k)))
        return out

    def spread1(full):
        out = []
        for k in range(1, nh):
            for h in range(2):
                part = full.at[xrows, ds(h * half + blk * cw, cw, 128)]
                out.append(send(part, part, at_z(NL * k)))
        return out

    def spread2(full):
        def left(k, idx, lo, n):
            part = full.at[xrows, ds(r * clw + lo, n, 128)]
            return part, part

        out = along_l(left)
        part = full.at[xrows, ds(half + r * clw, clw, 128)]
        return out + [send(part, part, at_x(k)) for k in range(1, nx)]

    def spread3(full):
        def right(k, idx, lo, n):
            part = full.at[:, ds(half + r * clw + lo, n, 128)]
            return part, part

        part = full.at[xrows, pl.ds(0, half)]
        out = [send(part, part, at_x(k)) for k in range(1, nx)]
        return out + along_l(right)

    def wait_all(copies):
        for cp in copies:
            cp.wait()

    def fold1(n, part):
        out = []
        for k in range(1, nx):
            theirs = ds((x + k) % nx * slots, slots, 16)
            out.append(send(part.at[theirs, pl.ds(0, half)], rx0.at[n, k - 1], at_x(k)))

        def right(k, idx, lo, size):
            src = part.at[:, ds(half + (r + k + NL) % NL * clw + lo, size, 128)]
            return src, rl1.at[n, idx, :, pl.ds(lo, size)]

        return out + along_l(right)

    def fold2(n, part, copies):
        wait_all(copies)
        for q in range(NL):
            cols = slice(q * clw, (q + 1) * clw)
            total = part[xrows, cols].astype(F32)
            for k in range(nx - 1):
                total += rx0[n, k, :, cols].astype(F32)
            s0[n, :, cols] = total.astype(BF16)
        own = ds(half + r * clw, clw, 128)
        for q in range(nx):
            rws = slice(q * slots, (q + 1) * slots)
            total = part[rws, own].astype(F32)
            for k in range(NL - 1):
                total += rl1[n, k, rws, :].astype(F32)
            s1[n, rws, :] = total.astype(BF16)

        def left(k, idx, lo, size):
            src = s0.at[n, :, ds((r + k + NL) % NL * clw + lo, size, 128)]
            return src, rl0.at[n, idx, :, pl.ds(lo, size)]

        out = along_l(left)
        for k in range(1, nx):
            theirs = ds((x + k) % nx * slots, slots, 16)
            out.append(send(s1.at[n, theirs, :], rx1.at[n, k - 1], at_x(k)))
        return out

    def fold3(n, copies):
        wait_all(copies)
        total = s0[n, :, ds(r * clw, clw, 128)].astype(F32)
        for k in range(NL - 1):
            total += rl0[n, k].astype(F32)
        tt[n, 0] = total.astype(BF16)
        total = s1[n, xrows, :].astype(F32)
        for k in range(nx - 1):
            total += rx1[n, k].astype(F32)
        tt[n, 1] = total.astype(BF16)
        out = []
        for k in range(1, nh):
            for h in range(2):
                src = tt.at[n, h, :, ds((zh + k) % nh * cw, cw, 128)]
                out.append(send(src, rh.at[n, h, k - 1], at_z(NL * k)))
        return out

    def fold4(n, copies):
        wait_all(copies)
        out = []
        for h in range(2):
            total = tt[n, h, :, ds(zh * cw, cw, 128)].astype(F32)
            for k in range(nh - 1):
                total += rh[n, h, k].astype(F32)
            out.append(total)
        return out

    for h in range(2):
        fx[xrows, ds(h * half + blk * cw, cw, 128)] = xs[:, h * cw : (h + 1) * cw].astype(BF16)
    wait_all(spread1(fx))
    wait_all(spread2(fx))
    cps = spread3(fx)
    for sends, full in zip(wsends, (wg, wu, wd)):
        for k, cp in enumerate(sends, 1):
            cp.wait()
            part = full.at[:, shard_of((y - k + ny) % ny * 2 + c)]
            wcore.append(send(part, part, partner))
    wait_all(wcore)
    wait_all(cps)

    xc[dp] = fx[:, shard_of(dp)]
    xcopies = []
    for k in range(1, ndp):
        i = (dp + k) % ndp
        xcopies.append(send(fx.at[:, shard_of(i)], xc.at[dp], at_dp(i)))

    gacc[...] = jnp.zeros_like(gacc)
    uacc[...] = jnp.zeros_like(uacc)

    @pl.loop(0, ndp)
    def _(i):
        cols = shard_of(i)
        block = fx[:, cols]
        gacc[...] += dot_nt(block, wg[:, cols])
        uacc[...] += dot_nt(block, wu[:, cols])

    pre = gacc[...]
    hid[...] = (jax.nn.sigmoid(pre) * pre * uacc[...]).astype(BF16)

    @pl.loop(0, ndp)
    def _(i):
        cols = shard_of(i)
        p1[:, cols] = dot_nn(hid[...], wd[:, cols]).astype(BF16)

    cps = fold1(0, p1)
    cps = fold2(0, p1, cps)
    cps = fold3(0, cps)
    sums = fold4(0, cps)
    for h in range(2):
        weight = gs[...]
        residual = weight * sums[h] - ts[:, h * cw : (h + 1) * cw]
        fc[xrows, ds(h * half + blk * cw, cw, 128)] = (weight * residual).astype(BF16)
    wait_all(spread1(fc))
    wait_all(spread2(fc))
    wait_all(spread3(fc))

    ga[...] = jnp.zeros_like(ga)

    @pl.loop(0, ndp)
    def _(i):
        cols = shard_of(i)
        ga[...] += dot_nt(fc[:, cols], wd[:, cols])

    pre = gacc[...]
    sig = jax.nn.sigmoid(pre)
    grad = ga[...]
    ggv = (grad * uacc[...] * (sig * (1.0 + pre * (1.0 - sig)))).astype(BF16)
    guv = (grad * (sig * pre)).astype(BF16)
    ga[...] = jnp.zeros_like(ga)
    hid[...] = ggv
    ua[...] = guv
    gga[dp] = jnp.zeros((rall, 2 * hp), BF16)
    gga[dp, :, 0:hloc] = ggv
    gga[dp, :, hp : hp + hloc] = guv
    gsends = [send(gga.at[dp], gga.at[dp], at_dp((y + k) % ny * 2 + c)) for k in range(1, ny)]
    gcore = [send(gga.at[dp], gga.at[dp], partner)]

    @pl.loop(0, ndp)
    def _(i):
        cols = shard_of(i)
        p2[:, cols] = (dot_nn(hid[...], wg[:, cols]) + dot_nn(ua[...], wu[:, cols])).astype(BF16)

    cps = fold1(1, p2)
    for k, cp in enumerate(gsends, 1):
        cp.wait()
        i = (y - k + ny) % ny * 2 + c
        gcore.append(send(gga.at[i], gga.at[i], partner))
    cps = fold2(1, p2, cps)
    wait_all(gcore)
    wait_all(xcopies)

    def weight_grad(lo, out_ref):
        def step(i, acc):
            return acc + dot_tn(gga[i, :, lo : lo + hp], xc[i])

        acc = lax.fori_loop(0, ndp, step, jnp.zeros((hp, dsh), F32))
        out_ref[...] = acc[0:hloc].astype(BF16)

    weight_grad(0, gg_out)
    weight_grad(hp, ug_out)
    cps = fold3(1, cps)
    sums = fold4(1, cps)

    rg[slots : slots + 8, :] = jnp.zeros((8, 2 * cw), F32)
    for h in range(2):
        rg[0:slots, h * cw : (h + 1) * cw] = sums[h]
    for k in range(nz):
        msg2[k] = rg[CAP * k : CAP * k + 8, :].astype(BF16)
    rmsg2[pl.ds(z, 1)] = msg2[pl.ds(z, 1)]
    wait_all([send(msg2.at[(z + k) % nz], rmsg2.at[z], at_z(k)) for k in range(1, nz)])
    keep = lax.broadcasted_iota(jnp.int32, (8, cw), 0) < CAP
    for k in range(nz):
        col = ((k % NL) * nh + k // NL) * cw
        for h in range(2):
            value = rmsg2[k, :, h * cw : (h + 1) * cw].astype(F32)
            rows[:, h * half + col : h * half + col + cw] = jnp.where(keep, value, 0.0)

    @pl.loop(0, ndp)
    def _(i):
        cols = shard_of(i)
        tg_out[:, cols] = dot_tn(sel[...].astype(BF16), rows[:, cols].astype(BF16)).astype(BF16)


def shards(nx, ndp, ne, tokens, expert_ids, gate_values, w_gate, w_up, w_down, target):
    tok_rows, width = tokens.shape
    hloc = w_gate.shape[1]
    nz = ne // nx
    nh = nz // NL
    slots, rall = nz * CAP, ne * CAP
    half = width // 2
    cw, dsh = half // nz, width // ndp
    clw = nh * cw
    hp = -(-hloc // 128) * 128
    vmem = pl.BlockSpec(memory_space=pltpu.VMEM)

    def buf(shape, dtype=BF16):
        return pltpu.VMEM(shape, dtype)

    scratch = [
        buf((hloc, width)), buf((hloc, width)), buf((hloc, width)),
        buf((rall, width)), buf((rall, width)), buf((rall, width)), buf((rall, width)),
        buf((ndp, rall, dsh)), buf((ndp, rall, 2 * hp)),
        buf((nz, 8, 2 * cw), F32), buf((nz, 8, 2 * cw), F32),
        buf((nz, 8, 2 * cw)), buf((nz, 8, 2 * cw)),
        buf((slots, 2 * cw), F32), buf((slots, 2 * cw), F32), buf((slots, cw), F32),
        buf((slots + 8, 2 * cw), F32), buf((8, width), F32), buf((8, tok_rows), F32),
        buf((rall, hloc), F32), buf((rall, hloc), F32), buf((rall, hloc)),
        buf((rall, hloc), F32), buf((rall, hloc)),
        buf((2, nx - 1, slots, half)), buf((2, NL - 1, rall, clw)),
        buf((2, NL - 1, slots, clw)), buf((2, nx - 1, slots, clw)),
        buf((2, 2, max(nh - 1, 1), slots, cw)),
        buf((2, slots, half)), buf((2, rall, clw)), buf((2, 2, slots, clw)),
        pltpu.SemaphoreType.DMA((2, 160)),
    ]
    token_grad, gate_grad, up_grad = pl.pallas_call(
        functools.partial(layer_kernel, nx, nz, ndp),
        out_shape=(
            jax.ShapeDtypeStruct((tok_rows, width), BF16),
            jax.ShapeDtypeStruct((hloc, dsh), BF16),
            jax.ShapeDtypeStruct((hloc, dsh), BF16),
        ),
        in_specs=[vmem] * 7,
        out_specs=(vmem,) * 3,
        scratch_shapes=scratch,
        compiler_params=pltpu.CompilerParams(
            collective_id=1, has_side_effects=True, vmem_limit_bytes=60 << 20
        ),
        name="expert_layer",
    )(tokens, target, expert_ids.T, gate_values.T, w_gate.T, w_up.T, w_down)
    return token_grad, gate_grad.T, up_grad.T


def solution(mesh, nx=NX):
    placed = (
        P(("dp", "expert"), None),
        P(("dp", "expert"), None),
        P(("dp", "expert"), None),
        P("dp", "expert"),
        P("dp", "expert"),
        P("expert", "dp"),
        P(("dp", "expert"), None),
    )
    return jax.shard_map(
        functools.partial(shards, nx, mesh.shape["dp"], mesh.shape["expert"]),
        mesh=mesh,
        in_specs=placed,
        out_specs=(P(("dp", "expert"), None), P("dp", "expert"), P("dp", "expert")),
        check_vma=False,
    )
```

```python
import functools

import jax
import jax.numpy as jnp
from jax import lax
from jax.experimental import pallas as pl
from jax.experimental.pallas import tpu as pltpu
from jax.sharding import PartitionSpec as P

MESH = pl.DeviceIdType.MESH
F32, BF16 = jnp.float32, jnp.bfloat16
CAP = 3
NX = 4
NL = 4


def dot_nn(a, b):
    return jnp.dot(a, b, preferred_element_type=F32)


def dot_nt(a, b):
    return lax.dot_general(a, b, (((1,), (1,)), ((), ())), preferred_element_type=F32)


def dot_tn(a, b):
    return lax.dot_general(a, b, (((0,), (0,)), ((), ())), preferred_element_type=F32)


def ds(start, size, unit):
    return pl.ds(pl.multiple_of(start, unit), size)


def layer_kernel(
    nx, nz, ndp, tok_ref, tgt_ref, ids_ref, gv_ref, wg_ref, wu_ref, wd_ref,
    rows_out, sel_out, gg_out, ug_out,
    wg, wu, wd, fx, fc, p1, p2, xc, gga,
    xmsg, xrcv, tmsg, trcv, msg2, rmsg2, xs, ts, gs, rg,
    gacc, uacc, hid, ua,
    rx0, rl1, rl0, rx1, rh, s0, s1, tt,
    sems,
):
    nh, ny = nz // NL, ndp // 2
    tok_rows, width = tok_ref.shape
    slots, rall = nz * CAP, nx * nz * CAP
    half = width // 2
    cw = half // nz
    clw = nh * cw
    dsh = width // ndp
    hloc = wg_ref.shape[0]
    hp = gga.shape[2] // 2

    dp, e = lax.axis_index("dp"), lax.axis_index("expert")
    y, c = dp // 2, dp % 2
    x, z = e // nz, e % nz
    r, zh = z % NL, z // NL
    blk = r * nh + zh

    def at_z(k):
        return (dp, x * nz + (z + k + nz) % nz)

    def at_x(k):
        return (dp, (x + k + nx) % nx * nz + z)

    def at_dp(i):
        return (i, e)

    def at_y(k):
        return (y + k + ny) % ny * 2 + c

    partner = at_dp(y * 2 + 1 - c)

    def rows_of(k):
        return ds((x + k + nx) % nx * slots, slots, 16)

    def class_of(k, h, lo=0, n=None):
        return ds(h * half + (r + k + NL) % NL * clw + lo, clw if n is None else n, 128)

    xrows = rows_of(0)
    used = [0]

    def send(src, dst, dev):
        n = used[0]
        used[0] += 1
        cp = pltpu.make_async_remote_copy(
            src_ref=src, dst_ref=dst, send_sem=sems.at[0, n], recv_sem=sems.at[1, n],
            device_id=dev, device_id_type=MESH,
        )
        cp.start()
        return cp

    def wait_all(copies):
        for cp in copies:
            cp.wait()

    barrier = pltpu.get_barrier_semaphore()
    peers = [at_z(k) for k in range(1, nz)] + [at_x(k) for k in range(1, nx)]
    peers += [at_dp((dp + k) % ndp) for k in range(1, ndp)]
    for dev in peers:
        pl.semaphore_signal(barrier, inc=1, device_id=dev, device_id_type=MESH)

    computed0 = ids_ref[0:1, :] < 1
    computed = jnp.logical_or(computed0, ids_ref[1:2, :] < 1)
    live = jnp.where(computed, 1.0, 0.0).astype(F32)
    gate = jnp.where(computed0, gv_ref[0:1, :], gv_ref[1:2, :])
    before = lax.broadcasted_iota(jnp.int32, (tok_rows, tok_rows), 0) < lax.broadcasted_iota(
        jnp.int32, (tok_rows, tok_rows), 1
    )
    live8 = jnp.broadcast_to(live, (8, tok_rows))
    slot = dot_nn(live8.astype(BF16), jnp.where(before, 1.0, 0.0).astype(BF16))
    row8 = lax.broadcasted_iota(jnp.int32, (8, tok_rows), 0).astype(F32)
    sel = jnp.where(slot == row8, live8, 0.0)
    sel_out[...] = sel
    selx = sel.astype(BF16)
    for k in range(nz):
        col = ((k % NL) * nh + k // NL) * cw
        for h in range(2):
            cols = slice(h * half + col, h * half + col + cw)
            xmsg[k, :, h * cw : (h + 1) * cw] = dot_nn(selx, tok_ref[:, cols]).astype(BF16)
    xrcv[pl.ds(z, 1)] = xmsg[pl.ds(z, 1)]

    pl.semaphore_wait(barrier, len(peers))

    tcps = [send(xmsg.at[(z + k) % nz], xrcv.at[z], at_z(k)) for k in range(1, nz)]

    def shard_of(i):
        return ds(i * dsh, dsh, 128)

    whole = ((wg_ref, wg), (wu_ref, wu), (wd_ref, wd))
    hh = hloc // 2
    wfirst, wrest = [None] * 3, []

    def weight_out(n):
        shard, full = whole[n]
        mine = full.at[:, shard_of(dp)]
        wfirst[n] = [send(shard, mine, at_dp(at_y(k))) for k in ((1, -1) if ny > 2 else (1,))]
        wrest.append(send(shard, mine, partner))

    def weight_on(n):
        full = whole[n][1]
        second = []
        for k, cp in zip((1, -1), wfirst[n]):
            cp.wait()
            cols = shard_of(at_y(-k))
            if ny > 2:
                part = full.at[pl.ds(0 if k == 1 else hh, hh), cols]
                second.append(send(part, part, at_dp(at_y(k))))
            part = full.at[:, cols]
            wrest.append(send(part, part, partner))
        return second

    def weight_end(n, second):
        wait_all(second)
        if ny > 2:
            part = whole[n][1].at[:, shard_of(at_y(2))]
            wrest.append(send(part, part, partner))

    weight_out(0)
    weight_out(1)
    for shard, full in whole:
        full[:, shard_of(dp)] = shard[...]

    gsel = sel * gate
    g0 = jnp.sum(gsel[0:1], axis=1, keepdims=True)
    g1 = jnp.sum(gsel[1:2], axis=1, keepdims=True)
    g2 = jnp.sum(gsel[2:3], axis=1, keepdims=True)
    rowc = lax.broadcasted_iota(jnp.int32, (8, cw), 0)
    gleft = jnp.where(rowc == 3, g0, jnp.where(rowc == 4, g2, 0.0))
    gright = jnp.where(rowc == 3, g1, 0.0)
    keep3 = rowc < CAP
    for k in range(nz):
        col = ((k % NL) * nh + k // NL) * cw
        for h, extra in ((0, gleft), (1, gright)):
            cols = slice(h * half + col, h * half + col + cw)
            piece = dot_nn(selx, tgt_ref[:, cols])
            tmsg[k, :, h * cw : (h + 1) * cw] = jnp.where(keep3, piece, extra)
    trcv[pl.ds(z, 1)] = tmsg[pl.ds(z, 1)]

    def along_l(ref_of):
        out = []
        for idx, k in enumerate((1, -1)):
            src, dst = ref_of(k, idx, 0, clw)
            out.append(send(src, dst, at_z(k)))
        for k, lo in ((2, 0), (-2, clw // 2)):
            src, dst = ref_of(k, 2, lo, clw // 2)
            out.append(send(src, dst, at_z(k)))
        return out

    far = sorted(range(1, nh), key=lambda k: -min(k, nh - k))
    xsteps = list(range(1, nx))

    def spread1(full):
        out = []
        for k in far:
            for h in range(2):
                part = full.at[xrows, ds(h * half + blk * cw, cw, 128)]
                out.append(send(part, part, at_z(NL * k)))
        return out

    def spread2(full, copies):
        wait_all(copies)

        def l_send(rws, h):
            def ref_of(k, idx, lo, n):
                part = full.at[rws, class_of(0, h, lo, n)]
                return part, part

            return along_l(ref_of)

        def x_send(k, h):
            part = full.at[xrows, class_of(k, h)]
            return [send(part, part, at_x(d)) for d in xsteps]

        first = l_send(xrows, 0)
        second = x_send(0, 1)
        last = x_send(0, 0) + l_send(xrows, 1)
        for q in range(3):
            if q < 2:
                first[q].wait()
            else:
                wait_all(first[2:])
            last += x_send((-1, 1, 2)[q], 0)
            if q < nx - 1:
                second[q].wait()
                last += l_send(rows_of(-xsteps[q]), 1)
        return last

    lsteps = (1, -1, 2, 0)
    xorder = xsteps + [0]

    def fold_right(n, part):
        out = []
        for q, d in enumerate(xorder):

            def ref_of(k, idx, lo, size):
                return part.at[rows_of(d), class_of(k, 1, lo, size)], rl1.at[n, q, idx, :, pl.ds(lo, size)]

            out.append(along_l(ref_of))
        return out

    def fold_left(n, part, q):
        cols = class_of(lsteps[q], 0)
        return [send(part.at[rows_of(k), cols], rx0.at[n, k - 1, q], at_x(k)) for k in xsteps]

    def fold2(n, part, left, right):
        out = []
        for q in range(NL):
            if q < nx:
                wait_all(right[q])
                total = part[rows_of(xorder[q]), class_of(0, 1)].astype(F32)
                for k in range(NL - 1):
                    total += rl1[n, q, k].astype(F32)
                s1[n, q] = total.astype(BF16)
                if xorder[q]:
                    out.append(send(s1.at[n, q], rx1.at[n, q], at_x(xorder[q])))
            wait_all(left[q])
            total = part[xrows, class_of(lsteps[q], 0)].astype(F32)
            for k in range(nx - 1):
                total += rx0[n, k, q].astype(F32)
            s0[n, q] = total.astype(BF16)
            if q < 2:
                out.append(send(s0.at[n, q], rl0.at[n, q], at_z(lsteps[q])))
            elif q == 2:
                for k, lo in ((2, 0), (-2, clw // 2)):
                    cols = pl.ds(lo, clw // 2)
                    out.append(send(s0.at[n, q, :, cols], rl0.at[n, q, :, cols], at_z(k)))
        return out

    def fold3(n, copies):
        wait_all(copies)
        total = s0[n, NL - 1].astype(F32)
        for k in range(NL - 1):
            total += rl0[n, k].astype(F32)
        tt[n, 0] = total.astype(BF16)
        total = s1[n, nx - 1].astype(F32)
        for k in range(nx - 1):
            total += rx1[n, k].astype(F32)
        tt[n, 1] = total.astype(BF16)
        out = []
        for k in far:
            for h in range(2):
                src = tt.at[n, h, :, ds((zh + k) % nh * cw, cw, 128)]
                out.append(send(src, rh.at[n, h, k - 1], at_z(NL * k)))
        return out

    def fold4(n, copies):
        wait_all(copies)
        out = []
        for h in range(2):
            total = tt[n, h, :, ds(zh * cw, cw, 128)].astype(F32)
            for k in range(nh - 1):
                total += rh[n, h, k].astype(F32)
            out.append(total)
        return out

    wait_all(tcps)
    for k in range(nz):
        xs[CAP * k : CAP * k + 3, :] = xrcv[k].astype(F32)[0:3]
    for h in range(2):
        fx[xrows, ds(h * half + blk * cw, cw, 128)] = xs[:, h * cw : (h + 1) * cw].astype(BF16)
    cps = spread1(fx)
    second = weight_on(0)
    weight_out(2)
    cps = spread2(fx, cps)
    tcps = [send(tmsg.at[(z + k) % nz], trcv.at[z], at_z(k)) for k in range(1, nz)]
    seconds = [second, weight_on(1)]
    seconds.append(weight_on(2))
    for n in range(3):
        weight_end(n, seconds[n])
    wait_all(cps)
    wait_all(wrest)

    xc[dp] = fx[:, shard_of(dp)]
    xcopies = []
    for k in range(1, ndp):
        i = (dp + k) % ndp
        xcopies.append(send(fx.at[:, shard_of(i)], xc.at[dp], at_dp(i)))

    gacc[...] = dot_nt(fx[...], wg[...])
    uacc[...] = dot_nt(fx[...], wu[...])
    pre = gacc[...]
    hid[...] = (jax.nn.sigmoid(pre) * pre * uacc[...]).astype(BF16)

    def produce(n, part, block):
        for k in lsteps:
            cols = class_of(k, 1)
            part[:, cols] = block(cols).astype(BF16)
        right = fold_right(n, part)
        left = []
        for q, k in enumerate(lsteps):
            cols = class_of(k, 0)
            part[:, cols] = block(cols).astype(BF16)
            left.append(fold_left(n, part, q))
        return left, right

    left, right = produce(0, p1, lambda cols: dot_nn(hid[...], wd[:, cols]))
    wait_all(tcps)
    for k in range(nz):
        b = CAP * k
        ts[b : b + 3, :] = trcv[k, 0:3, :]
        gs[b : b + 1, :] = trcv[k, 3:4, 0:cw]
        gs[b + 1 : b + 2, :] = trcv[k, 3:4, cw : 2 * cw]
        gs[b + 2 : b + 3, :] = trcv[k, 4:5, 0:cw]
    cps = fold2(0, p1, left, right)
    cps = fold3(0, cps)
    sums = fold4(0, cps)
    for h in range(2):
        weight = gs[...]
        residual = weight * sums[h] - ts[:, h * cw : (h + 1) * cw]
        fc[xrows, ds(h * half + blk * cw, cw, 128)] = (weight * residual).astype(BF16)
    cps = spread1(fc)
    cps = spread2(fc, cps)
    wait_all(cps)

    grad = dot_nt(fc[...], wd[...])
    pre = gacc[...]
    sig = jax.nn.sigmoid(pre)
    hid[...] = (grad * uacc[...] * (sig * (1.0 + pre * (1.0 - sig)))).astype(BF16)
    ua[...] = (grad * (sig * pre)).astype(BF16)
    if hp > hloc:
        gga[dp] = jnp.zeros((rall, 2 * hp), BF16)
    gga[dp, :, 0:hloc] = hid[...]
    gga[dp, :, hp : hp + hloc] = ua[...]
    gsends = [send(gga.at[dp], gga.at[dp], at_dp(at_y(k))) for k in range(1, ny)]
    gcore = [send(gga.at[dp], gga.at[dp], partner)]

    left, right = produce(
        1, p2, lambda cols: dot_nn(hid[...], wg[:, cols]) + dot_nn(ua[...], wu[:, cols])
    )
    cps = fold2(1, p2, left, right)
    for k, cp in enumerate(gsends, 1):
        cp.wait()
        i = at_y(-k)
        gcore.append(send(gga.at[i], gga.at[i], partner))
    cps = fold3(1, cps)
    wait_all(gcore)
    wait_all(xcopies)

    cb = min(256, dsh)
    for lo, out_ref in ((0, gg_out), (hp, ug_out)):
        for b in range(0, dsh, cb):
            lhs = gga[:, :, lo : lo + hp].reshape(ndp * rall, hp)
            rhs = xc[:, :, b : b + cb].reshape(ndp * rall, cb)
            out_ref[:, b : b + cb] = dot_tn(lhs, rhs)[0:hloc].astype(BF16)
    sums = fold4(1, cps)

    rg[slots : slots + 8, :] = jnp.zeros((8, 2 * cw), F32)
    for h in range(2):
        rg[0:slots, h * cw : (h + 1) * cw] = sums[h]
    for k in range(nz):
        msg2[k] = rg[CAP * k : CAP * k + 8, :].astype(BF16)
    rmsg2[pl.ds(z, 1)] = msg2[pl.ds(z, 1)]
    wait_all([send(msg2.at[(z + k) % nz], rmsg2.at[z], at_z(k)) for k in range(1, nz)])
    for k in range(nz):
        col = ((k % NL) * nh + k // NL) * cw
        for h in range(2):
            value = rmsg2[k, :, h * cw : (h + 1) * cw].astype(F32)
            value = jnp.where(keep3, value, 0.0)
            rows_out[:, h * half + col : h * half + col + cw] = value.astype(BF16)


def finish_kernel(rows_ref, sel_ref, gg_ref, ug_ref, tg_out, gg_out, ug_out):
    tg_out[...] = dot_tn(sel_ref[...].astype(BF16), rows_ref[...]).astype(BF16)
    gg_out[...] = gg_ref[...]
    ug_out[...] = ug_ref[...]


def shards(nx, ndp, ne, tokens, expert_ids, gate_values, w_gate, w_up, w_down, target):
    tok_rows, width = tokens.shape
    hloc = w_gate.shape[1]
    nz = ne // nx
    nh = nz // NL
    slots, rall = nz * CAP, ne * CAP
    half = width // 2
    cw, dsh = half // nz, width // ndp
    clw = nh * cw
    hp = -(-hloc // 128) * 128
    vmem = pl.BlockSpec(memory_space=pltpu.VMEM)

    def buf(shape, dtype=BF16):
        return pltpu.VMEM(shape, dtype)

    scratch = [
        buf((hloc, width)), buf((hloc, width)), buf((hloc, width)),
        buf((rall, width)), buf((rall, width)), buf((rall, width)), buf((rall, width)),
        buf((ndp, rall, dsh)), buf((ndp, rall, 2 * hp)),
        buf((nz, 8, 2 * cw)), buf((nz, 8, 2 * cw)),
        buf((nz, 8, 2 * cw), F32), buf((nz, 8, 2 * cw), F32),
        buf((nz, 8, 2 * cw)), buf((nz, 8, 2 * cw)),
        buf((slots, 2 * cw), F32), buf((slots, 2 * cw), F32), buf((slots, cw), F32),
        buf((slots + 8, 2 * cw), F32),
        buf((rall, hloc), F32), buf((rall, hloc), F32), buf((rall, hloc)), buf((rall, hloc)),
        buf((2, nx - 1, NL, slots, clw)), buf((2, nx, NL - 1, slots, clw)),
        buf((2, NL - 1, slots, clw)), buf((2, nx - 1, slots, clw)),
        buf((2, 2, max(nh - 1, 1), slots, cw)),
        buf((2, NL, slots, clw)), buf((2, nx, slots, clw)), buf((2, 2, slots, clw)),
        pltpu.SemaphoreType.DMA((2, 320)),
    ]
    shapes = (
        jax.ShapeDtypeStruct((hloc, dsh), BF16),
        jax.ShapeDtypeStruct((hloc, dsh), BF16),
    )
    rows, sel, gate_grad, up_grad = pl.pallas_call(
        functools.partial(layer_kernel, nx, nz, ndp),
        out_shape=(
            jax.ShapeDtypeStruct((8, width), BF16),
            jax.ShapeDtypeStruct((8, tok_rows), F32),
        ) + shapes,
        in_specs=[vmem] * 7,
        out_specs=(vmem,) * 4,
        scratch_shapes=scratch,
        compiler_params=pltpu.CompilerParams(
            collective_id=1, has_side_effects=True, vmem_limit_bytes=60 << 20
        ),
        name="expert_layer",
    )(tokens, target, expert_ids.T, gate_values.T, w_gate.T, w_up.T, w_down)
    token_grad, gate_grad, up_grad = pl.pallas_call(
        finish_kernel,
        out_shape=(jax.ShapeDtypeStruct((tok_rows, width), BF16),) + shapes,
        in_specs=[vmem] * 4,
        out_specs=(vmem,) * 3,
        name="finish",
    )(rows, sel, gate_grad, up_grad)
    return token_grad, gate_grad.T, up_grad.T


def solution(mesh, nx=NX):
    placed = (
        P(("dp", "expert"), None),
        P(("dp", "expert"), None),
        P(("dp", "expert"), None),
        P("dp", "expert"),
        P("dp", "expert"),
        P("expert", "dp"),
        P(("dp", "expert"), None),
    )
    return jax.shard_map(
        functools.partial(shards, nx, mesh.shape["dp"], mesh.shape["expert"]),
        mesh=mesh,
        in_specs=placed,
        out_specs=(P(("dp", "expert"), None), P("dp", "expert"), P("dp", "expert")),
        check_vma=False,
    )
```

```python
import functools

import jax
import jax.numpy as jnp
from jax import lax
from jax.experimental import pallas as pl
from jax.experimental.pallas import tpu as pltpu
from jax.sharding import PartitionSpec as P

MESH = pl.DeviceIdType.MESH
F32, BF16 = jnp.float32, jnp.bfloat16
CAP = 3
NX = 4
NL = 4


def dot_nn(a, b):
    return jnp.dot(a, b, preferred_element_type=F32)


def dot_nt(a, b):
    return lax.dot_general(a, b, (((1,), (1,)), ((), ())), preferred_element_type=F32)


def dot_tn(a, b):
    return lax.dot_general(a, b, (((0,), (0,)), ((), ())), preferred_element_type=F32)


def ds(start, size, unit):
    return pl.ds(pl.multiple_of(start, unit), size)


def layer_kernel(
    nx, nz, ndp, tok_ref, tgt_ref, ids_ref, gv_ref, wg_ref, wu_ref, wd_ref,
    rows_out, sel_out, gg_out, ug_out,
    wg, wu, wd, fx, fc, p1, p2, xc, gga,
    xmsg, xrcv, tmsg, trcv, msg2, rmsg2, xs, ts, gs, rg,
    gacc, uacc, hid, ua,
    rx0, rl1, rl0, rx1, rh, s0, s1, tt,
    sems,
):
    nh, ny = nz // NL, ndp // 2
    tok_rows, width = tok_ref.shape
    slots, rall = nz * CAP, nx * nz * CAP
    half = width // 2
    cw = half // nz
    clw = nh * cw
    dsh = width // ndp
    hloc = wg_ref.shape[0]
    hp = gga.shape[2] // 2

    dp, e = lax.axis_index("dp"), lax.axis_index("expert")
    y, c = dp // 2, dp % 2
    x, z = e // nz, e % nz
    r, zh = z % NL, z // NL
    blk = r * nh + zh

    def at_z(k):
        return (dp, x * nz + (z + k + nz) % nz)

    def at_x(k):
        return (dp, (x + k + nx) % nx * nz + z)

    def at_dp(i):
        return (i, e)

    def at_y(k):
        return (y + k + ny) % ny * 2 + c

    partner = at_dp(y * 2 + 1 - c)

    def rows_of(k):
        return ds((x + k + nx) % nx * slots, slots, 16)

    def class_of(k, h, lo=0, n=None):
        return ds(h * half + (r + k + NL) % NL * clw + lo, clw if n is None else n, 128)

    xrows = rows_of(0)
    used = [0]

    def send(src, dst, dev):
        n = used[0]
        used[0] += 1
        cp = pltpu.make_async_remote_copy(
            src_ref=src, dst_ref=dst, send_sem=sems.at[0, n], recv_sem=sems.at[1, n],
            device_id=dev, device_id_type=MESH,
        )
        cp.start()
        return cp

    def wait_all(copies):
        for cp in copies:
            cp.wait()

    barrier = pltpu.get_barrier_semaphore()
    peers = [at_z(k) for k in range(1, nz)] + [at_x(k) for k in range(1, nx)]
    peers += [at_dp((dp + k) % ndp) for k in range(1, ndp)]
    for dev in peers:
        pl.semaphore_signal(barrier, inc=1, device_id=dev, device_id_type=MESH)

    computed0 = ids_ref[0:1, :] < 1
    computed = jnp.logical_or(computed0, ids_ref[1:2, :] < 1)
    live = jnp.where(computed, 1.0, 0.0).astype(F32)
    gate = jnp.where(computed0, gv_ref[0:1, :], gv_ref[1:2, :])
    before = lax.broadcasted_iota(jnp.int32, (tok_rows, tok_rows), 0) < lax.broadcasted_iota(
        jnp.int32, (tok_rows, tok_rows), 1
    )
    live8 = jnp.broadcast_to(live, (8, tok_rows))
    slot = dot_nn(live8.astype(BF16), jnp.where(before, 1.0, 0.0).astype(BF16))
    row8 = lax.broadcasted_iota(jnp.int32, (8, tok_rows), 0).astype(F32)
    sel = jnp.where(slot == row8, live8, 0.0)
    sel_out[...] = sel
    selx = sel.astype(BF16)
    for q in range(NL):
        for h in range(2):
            cols = slice(h * half + q * clw, h * half + (q + 1) * clw)
            piece = dot_nn(selx, tok_ref[:, cols])[0:4].astype(BF16)
            xmsg[q, :, h * clw : (h + 1) * clw] = piece
    xrcv[pl.ds(z, 1)] = xmsg[pl.ds(r, 1)]

    pl.semaphore_wait(barrier, len(peers))

    tcps = [send(xmsg.at[(z + k) % NL], xrcv.at[z], at_z(k)) for k in range(1, nz)]

    def shard_of(i):
        return ds(i * dsh, dsh, 128)

    whole = ((wg_ref, wg), (wu_ref, wu), (wd_ref, wd))
    hh = hloc // 2
    wfirst, wrest = [None] * 3, []

    def weight_out(n):
        shard, full = whole[n]
        mine = full.at[:, shard_of(dp)]
        wfirst[n] = [send(shard, mine, at_dp(at_y(k))) for k in ((1, -1) if ny > 2 else (1,))]
        wrest.append(send(shard, mine, partner))

    def weight_on(n):
        full = whole[n][1]
        second = []
        for k, cp in zip((1, -1), wfirst[n]):
            cp.wait()
            cols = shard_of(at_y(-k))
            if ny > 2:
                part = full.at[pl.ds(0 if k == 1 else hh, hh), cols]
                second.append(send(part, part, at_dp(at_y(k))))
            part = full.at[:, cols]
            wrest.append(send(part, part, partner))
        return second

    def weight_end(n, second):
        wait_all(second)
        if ny > 2:
            part = whole[n][1].at[:, shard_of(at_y(2))]
            wrest.append(send(part, part, partner))

    weight_out(0)
    weight_out(1)
    for shard, full in whole:
        full[:, shard_of(dp)] = shard[...]

    gsel = sel * gate
    g0 = jnp.sum(gsel[0:1], axis=1, keepdims=True)
    g1 = jnp.sum(gsel[1:2], axis=1, keepdims=True)
    g2 = jnp.sum(gsel[2:3], axis=1, keepdims=True)
    rowc = lax.broadcasted_iota(jnp.int32, (8, cw), 0)
    gleft = jnp.where(rowc == 3, g0, jnp.where(rowc == 4, g2, 0.0))
    gright = jnp.where(rowc == 3, g1, 0.0)
    keep3 = rowc < CAP
    for k in range(nz):
        col = ((k % NL) * nh + k // NL) * cw
        for h, extra in ((0, gleft), (1, gright)):
            cols = slice(h * half + col, h * half + col + cw)
            piece = dot_nn(selx, tgt_ref[:, cols])
            tmsg[k, :, h * cw : (h + 1) * cw] = jnp.where(keep3, piece, extra)
    trcv[pl.ds(z, 1)] = tmsg[pl.ds(z, 1)]

    def along_l(ref_of):
        out = []
        for idx, k in enumerate((1, -1)):
            src, dst = ref_of(k, idx, 0, clw)
            out.append(send(src, dst, at_z(k)))
        for k, lo in ((2, 0), (-2, clw // 2)):
            src, dst = ref_of(k, 2, lo, clw // 2)
            out.append(send(src, dst, at_z(k)))
        return out

    far = sorted(range(1, nh), key=lambda k: -min(k, nh - k))
    xsteps = list(range(1, nx))

    def spread1(full):
        out = []
        for k in far:
            for h in range(2):
                part = full.at[xrows, ds(h * half + blk * cw, cw, 128)]
                out.append(send(part, part, at_z(NL * k)))
        return out

    def spread2(full, between=()):
        def l_send(rws, h):
            def ref_of(k, idx, lo, n):
                part = full.at[rws, class_of(0, h, lo, n)]
                return part, part

            return along_l(ref_of)

        def x_send(k, h):
            part = full.at[xrows, class_of(k, h)]
            return [send(part, part, at_x(d)) for d in xsteps]

        first = l_send(xrows, 0)
        second = x_send(0, 1)
        last = x_send(0, 0) + l_send(xrows, 1)
        for q in range(3):
            if q < len(between):
                between[q]()
            if q < 2:
                first[q].wait()
            else:
                wait_all(first[2:])
            last += x_send((-1, 1, 2)[q], 0)
            if q < nx - 1:
                second[q].wait()
                last += l_send(rows_of(-xsteps[q]), 1)
        return last

    lsteps = (1, -1, 2, 0)
    xorder = xsteps + [0]

    def fold_right(n, part):
        out = []
        for q, d in enumerate(xorder):

            def ref_of(k, idx, lo, size):
                return part.at[rows_of(d), class_of(k, 1, lo, size)], rl1.at[n, q, idx, :, pl.ds(lo, size)]

            out.append(along_l(ref_of))
        return out

    def fold_left(n, part, q):
        cols = class_of(lsteps[q], 0)
        return [send(part.at[rows_of(k), cols], rx0.at[n, k - 1, q], at_x(k)) for k in xsteps]

    def fold2(n, part, left, right):
        out = []
        for q in range(NL):
            if q < nx:
                wait_all(right[q])
                total = part[rows_of(xorder[q]), class_of(0, 1)].astype(F32)
                for k in range(NL - 1):
                    total += rl1[n, q, k].astype(F32)
                s1[n, q] = total.astype(BF16)
                if xorder[q]:
                    out.append(send(s1.at[n, q], rx1.at[n, q], at_x(xorder[q])))
            wait_all(left[q])
            total = part[xrows, class_of(lsteps[q], 0)].astype(F32)
            for k in range(nx - 1):
                total += rx0[n, k, q].astype(F32)
            s0[n, q] = total.astype(BF16)
            if q < 2:
                out.append(send(s0.at[n, q], rl0.at[n, q], at_z(lsteps[q])))
            elif q == 2:
                for k, lo in ((2, 0), (-2, clw // 2)):
                    cols = pl.ds(lo, clw // 2)
                    out.append(send(s0.at[n, q, :, cols], rl0.at[n, q, :, cols], at_z(k)))
        return out

    def class_sums(n, copies):
        wait_all(copies)
        left = s0[n, NL - 1].astype(F32)
        for k in range(NL - 1):
            left += rl0[n, k].astype(F32)
        right = s1[n, nx - 1].astype(F32)
        for k in range(nx - 1):
            right += rx1[n, k].astype(F32)
        return left, right

    def fold3(n, copies):
        for h, total in enumerate(class_sums(n, copies)):
            tt[n, h] = total.astype(BF16)
        out = []
        for k in far:
            for h in range(2):
                src = tt.at[n, h, :, ds((zh + k) % nh * cw, cw, 128)]
                out.append(send(src, rh.at[n, h, k - 1], at_z(NL * k)))
        return out

    def fold4(n, copies):
        wait_all(copies)
        out = []
        for h in range(2):
            total = tt[n, h, :, ds(zh * cw, cw, 128)].astype(F32)
            for k in range(nh - 1):
                total += rh[n, h, k].astype(F32)
            out.append(total)
        return out

    seconds = [weight_on(0)]
    weight_out(2)
    wait_all(tcps)
    for k in range(nz):
        xs[CAP * k : CAP * k + 3, :] = xrcv[k].astype(F32)[0:3]
    for h in range(2):
        fx[xrows, class_of(0, h)] = xs[:, h * clw : (h + 1) * clw].astype(BF16)
    cps = spread2(
        fx,
        (
            lambda: seconds.append(weight_on(1)),
            lambda: weight_end(0, seconds[0]),
            lambda: seconds.append(weight_on(2)),
        ),
    )
    tcps = [send(tmsg.at[(z + k) % nz], trcv.at[z], at_z(k)) for k in range(1, nz)]
    weight_end(1, seconds[1])
    weight_end(2, seconds[2])
    wait_all(cps)
    wait_all(wrest)

    xc[dp] = fx[:, shard_of(dp)]
    xcopies = []
    for k in range(1, ndp):
        i = (dp + k) % ndp
        xcopies.append(send(fx.at[:, shard_of(i)], xc.at[dp], at_dp(i)))

    gacc[...] = dot_nt(fx[...], wg[...])
    uacc[...] = dot_nt(fx[...], wu[...])
    pre = gacc[...]
    hid[...] = (jax.nn.sigmoid(pre) * pre * uacc[...]).astype(BF16)

    def produce(n, part, block):
        for k in lsteps:
            cols = class_of(k, 1)
            part[:, cols] = block(cols).astype(BF16)
        right = fold_right(n, part)
        left = []
        for q, k in enumerate(lsteps):
            cols = class_of(k, 0)
            part[:, cols] = block(cols).astype(BF16)
            left.append(fold_left(n, part, q))
        return left, right

    left, right = produce(0, p1, lambda cols: dot_nn(hid[...], wd[:, cols]))
    wait_all(tcps)
    for k in range(nz):
        b = CAP * k
        ts[b : b + 3, :] = trcv[k, 0:3, :]
        gs[b : b + 1, :] = trcv[k, 3:4, 0:cw]
        gs[b + 1 : b + 2, :] = trcv[k, 3:4, cw : 2 * cw]
        gs[b + 2 : b + 3, :] = trcv[k, 4:5, 0:cw]
    cps = fold2(0, p1, left, right)
    cps = fold3(0, cps)
    sums = fold4(0, cps)
    for h in range(2):
        weight = gs[...]
        residual = weight * sums[h] - ts[:, h * cw : (h + 1) * cw]
        fc[xrows, ds(h * half + blk * cw, cw, 128)] = (weight * residual).astype(BF16)
    wait_all(spread1(fc))
    wait_all(spread2(fc))

    grad = dot_nt(fc[...], wd[...])
    pre = gacc[...]
    sig = jax.nn.sigmoid(pre)
    hid[...] = (grad * uacc[...] * (sig * (1.0 + pre * (1.0 - sig)))).astype(BF16)
    ua[...] = (grad * (sig * pre)).astype(BF16)
    if hp > hloc:
        gga[dp] = jnp.zeros((rall, 2 * hp), BF16)
    gga[dp, :, 0:hloc] = hid[...]
    gga[dp, :, hp : hp + hloc] = ua[...]
    gsends = [send(gga.at[dp], gga.at[dp], at_dp(at_y(k))) for k in range(1, ny)]
    gcore = [send(gga.at[dp], gga.at[dp], partner)]

    left, right = produce(
        1, p2, lambda cols: dot_nn(hid[...], wg[:, cols]) + dot_nn(ua[...], wu[:, cols])
    )
    cps = fold2(1, p2, left, right)
    for k, cp in enumerate(gsends, 1):
        cp.wait()
        i = at_y(-k)
        gcore.append(send(gga.at[i], gga.at[i], partner))
    rg[slots : slots + 8, :] = jnp.zeros((8, 2 * clw), F32)
    for h, total in enumerate(class_sums(1, cps)):
        rg[0:slots, h * clw : (h + 1) * clw] = total
    for k in range(nz):
        msg2[k] = rg[CAP * k : CAP * k + 8, :][0:4].astype(BF16)
    rmsg2[pl.ds(z, 1)] = msg2[pl.ds(z, 1)]
    tcps = [send(msg2.at[(z + k) % nz], rmsg2.at[z], at_z(k)) for k in range(1, nz)]
    wait_all(gcore)
    wait_all(xcopies)

    cb = min(256, dsh)
    for lo, out_ref in ((0, gg_out), (hp, ug_out)):
        for b in range(0, dsh, cb):
            lhs = gga[:, :, lo : lo + hp].reshape(ndp * rall, hp)
            rhs = xc[:, :, b : b + cb].reshape(ndp * rall, cb)
            out_ref[:, b : b + cb] = dot_tn(lhs, rhs)[0:hloc].astype(BF16)

    wait_all(tcps)
    keep = lax.broadcasted_iota(jnp.int32, (4, clw), 0) < CAP
    for q in range(NL):
        for h in range(2):
            cols = slice(h * clw, (h + 1) * clw)
            total = rmsg2[q, :, cols].astype(F32)
            for k in range(1, nh):
                total += rmsg2[q + NL * k, :, cols].astype(F32)
            total = jnp.where(keep, total, 0.0)
            at = h * half + q * clw
            rows_out[:, at : at + clw] = jnp.concatenate([total, jnp.zeros_like(total)]).astype(BF16)


def finish_kernel(rows_ref, sel_ref, gg_ref, ug_ref, tg_out, gg_out, ug_out):
    tg_out[...] = dot_tn(sel_ref[...].astype(BF16), rows_ref[...]).astype(BF16)
    gg_out[...] = gg_ref[...]
    ug_out[...] = ug_ref[...]


def shards(nx, ndp, ne, tokens, expert_ids, gate_values, w_gate, w_up, w_down, target):
    tok_rows, width = tokens.shape
    hloc = w_gate.shape[1]
    nz = ne // nx
    nh = nz // NL
    slots, rall = nz * CAP, ne * CAP
    half = width // 2
    cw, dsh = half // nz, width // ndp
    clw = nh * cw
    hp = -(-hloc // 128) * 128
    vmem = pl.BlockSpec(memory_space=pltpu.VMEM)

    def buf(shape, dtype=BF16):
        return pltpu.VMEM(shape, dtype)

    scratch = [
        buf((hloc, width)), buf((hloc, width)), buf((hloc, width)),
        buf((rall, width)), buf((rall, width)), buf((rall, width)), buf((rall, width)),
        buf((ndp, rall, dsh)), buf((ndp, rall, 2 * hp)),
        buf((NL, 4, 2 * clw)), buf((nz, 4, 2 * clw)),
        buf((nz, 8, 2 * cw), F32), buf((nz, 8, 2 * cw), F32),
        buf((nz, 4, 2 * clw)), buf((nz, 4, 2 * clw)),
        buf((slots, 2 * clw), F32), buf((slots, 2 * cw), F32), buf((slots, cw), F32),
        buf((slots + 8, 2 * clw), F32),
        buf((rall, hloc), F32), buf((rall, hloc), F32), buf((rall, hloc)), buf((rall, hloc)),
        buf((2, nx - 1, NL, slots, clw)), buf((2, nx, NL - 1, slots, clw)),
        buf((2, NL - 1, slots, clw)), buf((2, nx - 1, slots, clw)),
        buf((2, 2, max(nh - 1, 1), slots, cw)),
        buf((2, NL, slots, clw)), buf((2, nx, slots, clw)), buf((2, 2, slots, clw)),
        pltpu.SemaphoreType.DMA((2, 300)),
    ]
    shapes = (
        jax.ShapeDtypeStruct((hloc, dsh), BF16),
        jax.ShapeDtypeStruct((hloc, dsh), BF16),
    )
    rows, sel, gate_grad, up_grad = pl.pallas_call(
        functools.partial(layer_kernel, nx, nz, ndp),
        out_shape=(
            jax.ShapeDtypeStruct((8, width), BF16),
            jax.ShapeDtypeStruct((8, tok_rows), F32),
        ) + shapes,
        in_specs=[vmem] * 7,
        out_specs=(vmem,) * 4,
        scratch_shapes=scratch,
        compiler_params=pltpu.CompilerParams(
            collective_id=1, has_side_effects=True, vmem_limit_bytes=60 << 20
        ),
        name="expert_layer",
    )(tokens, target, expert_ids.T, gate_values.T, w_gate.T, w_up.T, w_down)
    token_grad, gate_grad, up_grad = pl.pallas_call(
        finish_kernel,
        out_shape=(jax.ShapeDtypeStruct((tok_rows, width), BF16),) + shapes,
        in_specs=[vmem] * 4,
        out_specs=(vmem,) * 3,
        name="finish",
    )(rows, sel, gate_grad, up_grad)
    return token_grad, gate_grad.T, up_grad.T


def solution(mesh, nx=NX):
    placed = (
        P(("dp", "expert"), None),
        P(("dp", "expert"), None),
        P(("dp", "expert"), None),
        P("dp", "expert"),
        P("dp", "expert"),
        P("expert", "dp"),
        P(("dp", "expert"), None),
    )
    return jax.shard_map(
        functools.partial(shards, nx, mesh.shape["dp"], mesh.shape["expert"]),
        mesh=mesh,
        in_specs=placed,
        out_specs=(P(("dp", "expert"), None), P("dp", "expert"), P("dp", "expert")),
        check_vma=False,
    )
```

```python
import functools

import jax
import jax.numpy as jnp
from jax import lax
from jax.experimental import pallas as pl
from jax.experimental.pallas import tpu as pltpu
from jax.sharding import PartitionSpec as P

MESH = pl.DeviceIdType.MESH
F32, BF16 = jnp.float32, jnp.bfloat16
CAP = 3
NX = 4
NL = 4


def dot_nn(a, b):
    return jnp.dot(a, b, preferred_element_type=F32)


def dot_nt(a, b):
    return lax.dot_general(a, b, (((1,), (1,)), ((), ())), preferred_element_type=F32)


def dot_tn(a, b):
    return lax.dot_general(a, b, (((0,), (0,)), ((), ())), preferred_element_type=F32)


def ds(start, size, unit):
    return pl.ds(pl.multiple_of(start, unit), size)


def layer_kernel(
    nx, nz, ndp, tok_hbm, tgt_hbm, ids_hbm, gv_hbm, wg_ref, wu_ref, wd_ref,
    rows_out, sel_out, gg_out, ug_out,
    wg, wu, wd, fx, fc, p1, p2, xc, gga,
    xmsg, xrcv, tmsg, trcv, msg2, rmsg2, xs, ts, gs, rg,
    gacc, uacc, hid, ua,
    rx0, rl1, rl0, rx1, rh, s0, s1, tt,
    tok_ref, tgt_ref, ids_ref, gv_ref, lsems, sems,
):
    nh, ny = nz // NL, ndp // 2
    tok_rows, width = tok_ref.shape
    slots, rall = nz * CAP, nx * nz * CAP
    half = width // 2
    cw = half // nz
    clw = nh * cw
    dsh = width // ndp
    hloc = wg_ref.shape[0]
    hp = gga.shape[2] // 2
    zfar = sorted(range(1, nz), key=lambda k: -min(k, nz - k))

    dp, e = lax.axis_index("dp"), lax.axis_index("expert")
    y, c = dp // 2, dp % 2
    x, z = e // nz, e % nz
    r, zh = z % NL, z // NL
    blk = r * nh + zh
    near = y * 2 // ny
    hoff = ((1 - near) * half, near * half)

    def at_z(k):
        return (dp, x * nz + (z + k + nz) % nz)

    def at_x(k):
        return (dp, (x + k + nx) % nx * nz + z)

    def at_dp(i):
        return (i, e)

    def at_y(k):
        return (y + k + ny) % ny * 2 + c

    partner = at_dp(y * 2 + 1 - c)

    def rows_of(k):
        return ds((x + k + nx) % nx * slots, slots, 16)

    def class_of(k, h, lo=0, n=None):
        return ds(hoff[h] + (r + k + NL) % NL * clw + lo, clw if n is None else n, 128)

    xrows = rows_of(0)
    used = [0]

    def send(src, dst, dev):
        n = used[0]
        used[0] += 1
        cp = pltpu.make_async_remote_copy(
            src_ref=src, dst_ref=dst, send_sem=sems.at[0, n], recv_sem=sems.at[1, n],
            device_id=dev, device_id_type=MESH,
        )
        cp.start()
        return cp

    def wait_all(copies):
        for cp in copies:
            cp.wait()

    barrier = pltpu.get_barrier_semaphore()
    peers = [at_z(k) for k in range(1, nz)] + [at_x(k) for k in range(1, nx)]
    peers += [at_dp((dp + k) % ndp) for k in range(1, ndp)]
    for dev in peers:
        pl.semaphore_signal(barrier, inc=1, device_id=dev, device_id_type=MESH)

    def shard_of(i):
        return ds(i * dsh, dsh, 128)

    pairs = (
        (ids_hbm, ids_ref), (gv_hbm, gv_ref), (tok_hbm, tok_ref), (tgt_hbm, tgt_ref),
        (wg_ref, wg.at[:, shard_of(dp)]), (wu_ref, wu.at[:, shard_of(dp)]),
        (wd_ref, wd.at[:, shard_of(dp)]),
    )
    loads = [pltpu.make_async_copy(a, b, lsems.at[n]) for n, (a, b) in enumerate(pairs)]
    for n in (0, 1, 2, 4, 5, 6, 3):
        loads[n].start()

    loads[0].wait()
    loads[1].wait()
    computed0 = ids_ref[0:1, :] < 1
    computed = jnp.logical_or(computed0, ids_ref[1:2, :] < 1)
    live = jnp.where(computed, 1.0, 0.0).astype(F32)
    gate = jnp.where(computed0, gv_ref[0:1, :], gv_ref[1:2, :])
    before = lax.broadcasted_iota(jnp.int32, (tok_rows, tok_rows), 0) < lax.broadcasted_iota(
        jnp.int32, (tok_rows, tok_rows), 1
    )
    live8 = jnp.broadcast_to(live, (8, tok_rows))
    slot = dot_nn(live8.astype(BF16), jnp.where(before, 1.0, 0.0).astype(BF16))
    row8 = lax.broadcasted_iota(jnp.int32, (8, tok_rows), 0).astype(F32)
    sel = jnp.where(slot == row8, live8, 0.0)
    sel_out[...] = sel
    selx = sel.astype(BF16)
    loads[2].wait()
    for q in range(NL):
        for h in range(2):
            cols = ds(hoff[h] + q * clw, clw, 128)
            piece = dot_nn(selx, tok_ref[:, cols])[0:4].astype(BF16)
            xmsg[q, :, h * clw : (h + 1) * clw] = piece
    xrcv[pl.ds(z, 1)] = xmsg[pl.ds(r, 1)]

    for n in (4, 5, 6):
        loads[n].wait()
    pl.semaphore_wait(barrier, len(peers))

    tcps = [send(xmsg.at[(z + k) % NL], xrcv.at[z], at_z(k)) for k in zfar]

    whole = (wg, wu, wd)
    hh = hloc // 2
    wfirst, wrest = [None] * 3, [[], [], []]

    def weight_out(n):
        mine = whole[n].at[:, shard_of(dp)]
        wfirst[n] = [send(mine, mine, at_dp(at_y(k))) for k in ((1, -1) if ny > 2 else (1,))]
        wrest[n].append(send(mine, mine, partner))

    def weight_on(n):
        second = []
        for k, cp in zip((1, -1), wfirst[n]):
            cp.wait()
            cols = shard_of(at_y(-k))
            if ny > 2:
                part = whole[n].at[pl.ds(0 if k == 1 else hh, hh), cols]
                second.append(send(part, part, at_dp(at_y(k))))
            part = whole[n].at[:, cols]
            wrest[n].append(send(part, part, partner))
        return second

    def weight_end(n, second):
        wait_all(second)
        if ny > 2:
            part = whole[n].at[:, shard_of(at_y(2))]
            wrest[n].append(send(part, part, partner))

    weight_out(0)
    weight_out(1)

    loads[3].wait()
    gsel = sel * gate
    g0 = jnp.sum(gsel[0:1], axis=1, keepdims=True)
    g1 = jnp.sum(gsel[1:2], axis=1, keepdims=True)
    g2 = jnp.sum(gsel[2:3], axis=1, keepdims=True)
    rowc = lax.broadcasted_iota(jnp.int32, (8, cw), 0)
    gleft = jnp.where(rowc == 3, g0, jnp.where(rowc == 4, g2, 0.0))
    gright = jnp.where(rowc == 3, g1, 0.0)
    keep3 = rowc < CAP
    for k in range(nz):
        col = ((k % NL) * nh + k // NL) * cw
        for h, extra in ((0, gleft), (1, gright)):
            cols = ds(hoff[h] + col, cw, 128)
            piece = dot_nn(selx, tgt_ref[:, cols])
            tmsg[k, :, h * cw : (h + 1) * cw] = jnp.where(keep3, piece, extra)
    trcv[pl.ds(z, 1)] = tmsg[pl.ds(z, 1)]

    def along_l(ref_of):
        out = []
        for idx, k in enumerate((1, -1)):
            src, dst = ref_of(k, idx, 0, clw)
            out.append(send(src, dst, at_z(k)))
        for k, lo in ((2, 0), (-2, clw // 2)):
            src, dst = ref_of(k, 2, lo, clw // 2)
            out.append(send(src, dst, at_z(k)))
        return out

    far = sorted(range(1, nh), key=lambda k: -min(k, nh - k))
    xsteps = list(range(1, nx))

    def spread1(full):
        out = []
        for k in far:
            for h in range(2):
                part = full.at[xrows, ds(hoff[h] + blk * cw, cw, 128)]
                out.append(send(part, part, at_z(NL * k)))
        return out

    def spread2(full, between=()):
        def l_send(rws, h):
            def ref_of(k, idx, lo, n):
                part = full.at[rws, class_of(0, h, lo, n)]
                return part, part

            return along_l(ref_of)

        def x_send(k, h):
            part = full.at[xrows, class_of(k, h)]
            return [send(part, part, at_x(d)) for d in xsteps]

        first = l_send(xrows, 0)
        second = x_send(0, 1)
        last = x_send(0, 0) + l_send(xrows, 1)
        for q in range(3):
            if q < len(between):
                between[q]()
            if q < 2:
                first[q].wait()
            else:
                wait_all(first[2:])
            last += x_send((-1, 1, 2)[q], 0)
            if q < nx - 1:
                second[q].wait()
                last += l_send(rows_of(-xsteps[q]), 1)
        return last

    lsteps = (1, -1, 2, 0)
    xorder = xsteps + [0]

    def fold_right(n, part):
        out = []
        for q, d in enumerate(xorder):

            def ref_of(k, idx, lo, size):
                return part.at[rows_of(d), class_of(k, 1, lo, size)], rl1.at[n, q, idx, :, pl.ds(lo, size)]

            out.append(along_l(ref_of))
        return out

    def fold_left(n, part, q):
        cols = class_of(lsteps[q], 0)
        return [send(part.at[rows_of(k), cols], rx0.at[n, k - 1, q], at_x(k)) for k in xsteps]

    def fold2(n, part, left, right):
        out = []
        for q in range(NL):
            if q < nx:
                wait_all(right[q])
                total = part[rows_of(xorder[q]), class_of(0, 1)].astype(F32)
                for k in range(NL - 1):
                    total += rl1[n, q, k].astype(F32)
                s1[n, q] = total.astype(BF16)
                if xorder[q]:
                    out.append(send(s1.at[n, q], rx1.at[n, q], at_x(xorder[q])))
            wait_all(left[q])
            total = part[xrows, class_of(lsteps[q], 0)].astype(F32)
            for k in range(nx - 1):
                total += rx0[n, k, q].astype(F32)
            s0[n, q] = total.astype(BF16)
            if q < 2:
                out.append(send(s0.at[n, q], rl0.at[n, q], at_z(lsteps[q])))
            elif q == 2:
                for k, lo in ((2, 0), (-2, clw // 2)):
                    cols = pl.ds(lo, clw // 2)
                    out.append(send(s0.at[n, q, :, cols], rl0.at[n, q, :, cols], at_z(k)))
        return out

    def class_sums(n, copies):
        wait_all(copies)
        left = s0[n, NL - 1].astype(F32)
        for k in range(NL - 1):
            left += rl0[n, k].astype(F32)
        right = s1[n, nx - 1].astype(F32)
        for k in range(nx - 1):
            right += rx1[n, k].astype(F32)
        return left, right

    def fold3(n, copies):
        for h, total in enumerate(class_sums(n, copies)):
            tt[n, h] = total.astype(BF16)
        out = []
        for k in far:
            for h in range(2):
                src = tt.at[n, h, :, ds((zh + k) % nh * cw, cw, 128)]
                out.append(send(src, rh.at[n, h, k - 1], at_z(NL * k)))
        return out

    def fold4(n, copies):
        wait_all(copies)
        out = []
        for h in range(2):
            total = tt[n, h, :, ds(zh * cw, cw, 128)].astype(F32)
            for k in range(nh - 1):
                total += rh[n, h, k].astype(F32)
            out.append(total)
        return out

    seconds = [weight_on(0)]
    wait_all(tcps)
    for k in range(nz):
        xs[CAP * k : CAP * k + 3, :] = xrcv[k].astype(F32)[0:3]
    for h in range(2):
        fx[xrows, class_of(0, h)] = xs[:, h * clw : (h + 1) * clw].astype(BF16)

    def up_then_down():
        seconds.append(weight_on(1))
        weight_out(2)

    cps = spread2(
        fx,
        (up_then_down, lambda: weight_end(0, seconds[0]), lambda: weight_end(1, seconds[1])),
    )
    tcps = [send(tmsg.at[(z + k) % nz], trcv.at[z], at_z(k)) for k in zfar]
    seconds.append(weight_on(2))
    wait_all(cps)
    wait_all(wrest[0] + wrest[1])

    xc[dp] = fx[:, shard_of(dp)]
    xcopies = []
    for k in range(1, ndp):
        i = (dp + k) % ndp
        xcopies.append(send(fx.at[:, shard_of(i)], xc.at[dp], at_dp(i)))

    gacc[...] = dot_nt(fx[...], wg[...])
    uacc[...] = dot_nt(fx[...], wu[...])
    pre = gacc[...]
    hid[...] = (jax.nn.sigmoid(pre) * pre * uacc[...]).astype(BF16)

    def produce_right(n, part, block):
        for k in lsteps:
            cols = class_of(k, 1)
            part[:, cols] = block(cols).astype(BF16)
        return fold_right(n, part)

    def produce_left(n, part, block):
        left = []
        for q, k in enumerate(lsteps):
            cols = class_of(k, 0)
            part[:, cols] = block(cols).astype(BF16)
            left.append(fold_left(n, part, q))
        return left

    def down(cols):
        return dot_nn(hid[...], wd[:, cols])

    wait_all(wrest[2])
    right = produce_right(0, p1, down)
    weight_end(2, seconds[2])
    wait_all(wrest[2][3 if ny > 2 else 2 :])
    left = produce_left(0, p1, down)
    wait_all(tcps)
    for k in range(nz):
        b = CAP * k
        ts[b : b + 3, :] = trcv[k, 0:3, :]
        gs[b : b + 1, :] = trcv[k, 3:4, 0:cw]
        gs[b + 1 : b + 2, :] = trcv[k, 3:4, cw : 2 * cw]
        gs[b + 2 : b + 3, :] = trcv[k, 4:5, 0:cw]
    cps = fold2(0, p1, left, right)
    cps = fold3(0, cps)
    sums = fold4(0, cps)
    for h in range(2):
        weight = gs[...]
        residual = weight * sums[h] - ts[:, h * cw : (h + 1) * cw]
        fc[xrows, ds(hoff[h] + blk * cw, cw, 128)] = (weight * residual).astype(BF16)
    wait_all(spread1(fc))
    wait_all(spread2(fc))

    grad = dot_nt(fc[...], wd[...])
    pre = gacc[...]
    sig = jax.nn.sigmoid(pre)
    hid[...] = (grad * uacc[...] * (sig * (1.0 + pre * (1.0 - sig)))).astype(BF16)
    ua[...] = (grad * (sig * pre)).astype(BF16)
    if hp > hloc:
        gga[dp] = jnp.zeros((rall, 2 * hp), BF16)
    gga[dp, :, 0:hloc] = hid[...]
    gga[dp, :, hp : hp + hloc] = ua[...]
    gsends = [send(gga.at[dp], gga.at[dp], at_dp(at_y(k))) for k in range(1, ny)]
    gcore = [send(gga.at[dp], gga.at[dp], partner)]

    def back(cols):
        return dot_nn(hid[...], wg[:, cols]) + dot_nn(ua[...], wu[:, cols])

    right = produce_right(1, p2, back)
    left = produce_left(1, p2, back)
    cps = fold2(1, p2, left, right)
    for k, cp in enumerate(gsends, 1):
        cp.wait()
        i = at_y(-k)
        gcore.append(send(gga.at[i], gga.at[i], partner))
    rg[slots : slots + 8, :] = jnp.zeros((8, 2 * clw), F32)
    for h, total in enumerate(class_sums(1, cps)):
        rg[0:slots, h * clw : (h + 1) * clw] = total
    for k in range(nz):
        msg2[k] = rg[CAP * k : CAP * k + 8, :][0:4].astype(BF16)
    rmsg2[pl.ds(z, 1)] = msg2[pl.ds(z, 1)]
    tcps = [send(msg2.at[(z + k) % nz], rmsg2.at[z], at_z(k)) for k in zfar]
    wait_all(gcore)
    wait_all(xcopies)

    cb = min(256, dsh)
    for lo, out_ref in ((0, gg_out), (hp, ug_out)):
        for b in range(0, dsh, cb):
            lhs = gga[:, :, lo : lo + hp].reshape(ndp * rall, hp)
            rhs = xc[:, :, b : b + cb].reshape(ndp * rall, cb)
            out_ref[:, b : b + cb] = dot_tn(lhs, rhs)[0:hloc].astype(BF16)

    wait_all(tcps)
    keep = lax.broadcasted_iota(jnp.int32, (4, clw), 0) < CAP
    for q in range(NL):
        for h in range(2):
            cols = slice(h * clw, (h + 1) * clw)
            total = rmsg2[q, :, cols].astype(F32)
            for k in range(1, nh):
                total += rmsg2[q + NL * k, :, cols].astype(F32)
            total = jnp.where(keep, total, 0.0)
            rows_out[:, ds(hoff[h] + q * clw, clw, 128)] = jnp.concatenate([total, jnp.zeros_like(total)]).astype(BF16)


def finish_kernel(rows_ref, sel_ref, gg_ref, ug_ref, tg_out, gg_out, ug_out):
    tg_out[...] = dot_tn(sel_ref[...].astype(BF16), rows_ref[...]).astype(BF16)
    gg_out[...] = gg_ref[...]
    ug_out[...] = ug_ref[...]


def shards(nx, ndp, ne, tokens, expert_ids, gate_values, w_gate, w_up, w_down, target):
    tok_rows, width = tokens.shape
    hloc = w_gate.shape[1]
    nz = ne // nx
    nh = nz // NL
    slots, rall = nz * CAP, ne * CAP
    half = width // 2
    cw, dsh = half // nz, width // ndp
    clw = nh * cw
    hp = -(-hloc // 128) * 128
    vmem = pl.BlockSpec(memory_space=pltpu.VMEM)

    def buf(shape, dtype=BF16):
        return pltpu.VMEM(shape, dtype)

    scratch = [
        buf((hloc, width)), buf((hloc, width)), buf((hloc, width)),
        buf((rall, width)), buf((rall, width)), buf((rall, width)), buf((rall, width)),
        buf((ndp, rall, dsh)), buf((ndp, rall, 2 * hp)),
        buf((NL, 4, 2 * clw)), buf((nz, 4, 2 * clw)),
        buf((nz, 8, 2 * cw), F32), buf((nz, 8, 2 * cw), F32),
        buf((nz, 4, 2 * clw)), buf((nz, 4, 2 * clw)),
        buf((slots, 2 * clw), F32), buf((slots, 2 * cw), F32), buf((slots, cw), F32),
        buf((slots + 8, 2 * clw), F32),
        buf((rall, hloc), F32), buf((rall, hloc), F32), buf((rall, hloc)), buf((rall, hloc)),
        buf((2, nx - 1, NL, slots, clw)), buf((2, nx, NL - 1, slots, clw)),
        buf((2, NL - 1, slots, clw)), buf((2, nx - 1, slots, clw)),
        buf((2, 2, max(nh - 1, 1), slots, cw)),
        buf((2, NL, slots, clw)), buf((2, nx, slots, clw)), buf((2, 2, slots, clw)),
        buf((tok_rows, width)), buf((tok_rows, width)),
        buf((2, tok_rows), jnp.int32), buf((2, tok_rows), F32),
        pltpu.SemaphoreType.DMA((7,)),
        pltpu.SemaphoreType.DMA((2, 300)),
    ]
    shapes = (
        jax.ShapeDtypeStruct((hloc, dsh), BF16),
        jax.ShapeDtypeStruct((hloc, dsh), BF16),
    )
    rows, sel, gate_grad, up_grad = pl.pallas_call(
        functools.partial(layer_kernel, nx, nz, ndp),
        out_shape=(
            jax.ShapeDtypeStruct((8, width), BF16),
            jax.ShapeDtypeStruct((8, tok_rows), F32),
        ) + shapes,
        in_specs=[pl.BlockSpec(memory_space=pl.ANY)] * 7,
        out_specs=(vmem,) * 4,
        scratch_shapes=scratch,
        compiler_params=pltpu.CompilerParams(
            collective_id=1, has_side_effects=True, vmem_limit_bytes=60 << 20
        ),
        name="expert_layer",
    )(tokens, target, expert_ids.T, gate_values.T, w_gate.T, w_up.T, w_down)
    token_grad, gate_grad, up_grad = pl.pallas_call(
        finish_kernel,
        out_shape=(jax.ShapeDtypeStruct((tok_rows, width), BF16),) + shapes,
        in_specs=[vmem] * 4,
        out_specs=(vmem,) * 3,
        name="finish",
    )(rows, sel, gate_grad, up_grad)
    return token_grad, gate_grad.T, up_grad.T


def solution(mesh, nx=NX):
    placed = (
        P(("dp", "expert"), None),
        P(("dp", "expert"), None),
        P(("dp", "expert"), None),
        P("dp", "expert"),
        P("dp", "expert"),
        P("expert", "dp"),
        P(("dp", "expert"), None),
    )
    return jax.shard_map(
        functools.partial(shards, nx, mesh.shape["dp"], mesh.shape["expert"]),
        mesh=mesh,
        in_specs=placed,
        out_specs=(P(("dp", "expert"), None), P("dp", "expert"), P("dp", "expert")),
        check_vma=False,
    )
```

```python
import functools

import jax
import jax.numpy as jnp
from jax import lax
from jax.experimental import pallas as pl
from jax.experimental.pallas import tpu as pltpu
from jax.sharding import PartitionSpec as P

MESH = pl.DeviceIdType.MESH
F32, BF16 = jnp.float32, jnp.bfloat16
CAP = 3
NX = 4
NL = 4


def dot_nn(a, b):
    return jnp.dot(a, b, preferred_element_type=F32)


def dot_nt(a, b):
    return lax.dot_general(a, b, (((1,), (1,)), ((), ())), preferred_element_type=F32)


def dot_tn(a, b):
    return lax.dot_general(a, b, (((0,), (0,)), ((), ())), preferred_element_type=F32)


def ds(start, size, unit):
    return pl.ds(pl.multiple_of(start, unit), size)


def layer_kernel(
    nx, nz, ndp, tok_hbm, tgt_hbm, ids_hbm, gv_hbm, wg_ref, wu_ref, wd_ref,
    rows_out, sel_out, gg_out, ug_out,
    wg, wu, wd, fx, fc, p1, p2, xc, gga,
    xmsg, xrcv, tmsg, trcv, msg2, rmsg2, xs, ts, gs, rg,
    gacc, uacc, hid, ua,
    rx0, rl1, rl0, rx1, rh, s0, s1, tt,
    tok_ref, tgt_ref, ids_ref, gv_ref, lsems, sems,
):
    nh, ny = nz // NL, ndp // 2
    tok_rows, width = tok_ref.shape
    slots, rall = nz * CAP, nx * nz * CAP
    half = width // 2
    cw = half // nz
    clw = nh * cw
    dsh = width // ndp
    hloc = wg_ref.shape[0]
    hp = gga.shape[2] // 2
    zfar = sorted(range(1, nz), key=lambda k: -min(k, nz - k))

    dp, e = lax.axis_index("dp"), lax.axis_index("expert")
    y, c = dp // 2, dp % 2
    x, z = e // nz, e % nz
    r, zh = z % NL, z // NL
    blk = r * nh + zh
    near = y * 2 // ny
    hoff = ((1 - near) * half, near * half)

    def at_z(k):
        return (dp, x * nz + (z + k + nz) % nz)

    def at_x(k):
        return (dp, (x + k + nx) % nx * nz + z)

    def at_dp(i):
        return (i, e)

    def at_y(k):
        return (y + k + ny) % ny * 2 + c

    partner = at_dp(y * 2 + 1 - c)

    def rows_of(k):
        return ds((x + k + nx) % nx * slots, slots, 16)

    def class_of(k, h, lo=0, n=None):
        return ds(hoff[h] + (r + k + NL) % NL * clw + lo, clw if n is None else n, 128)

    xrows = rows_of(0)
    used = [0]

    def send(src, dst, dev):
        n = used[0]
        used[0] += 1
        cp = pltpu.make_async_remote_copy(
            src_ref=src, dst_ref=dst, send_sem=sems.at[0, n], recv_sem=sems.at[1, n],
            device_id=dev, device_id_type=MESH,
        )
        cp.start()
        return cp

    def wait_all(copies):
        for cp in copies:
            cp.wait()

    barrier = pltpu.get_barrier_semaphore()
    peers = [at_z(k) for k in range(1, nz)] + [at_x(k) for k in range(1, nx)]
    peers += [at_dp((dp + k) % ndp) for k in range(1, ndp)]
    for dev in peers:
        pl.semaphore_signal(barrier, inc=1, device_id=dev, device_id_type=MESH)

    def shard_of(i):
        return ds(i * dsh, dsh, 128)

    pairs = (
        (ids_hbm, ids_ref), (gv_hbm, gv_ref), (tok_hbm, tok_ref), (tgt_hbm, tgt_ref),
        (wg_ref, wg.at[:, shard_of(dp)]), (wu_ref, wu.at[:, shard_of(dp)]),
        (wd_ref, wd.at[:, shard_of(dp)]),
    )
    loads = [pltpu.make_async_copy(a, b, lsems.at[n]) for n, (a, b) in enumerate(pairs)]
    for n in (0, 1, 2, 4, 5, 6, 3):
        loads[n].start()

    loads[0].wait()
    loads[1].wait()
    computed0 = ids_ref[0:1, :] < 1
    computed = jnp.logical_or(computed0, ids_ref[1:2, :] < 1)
    live = jnp.where(computed, 1.0, 0.0).astype(F32)
    gate = jnp.where(computed0, gv_ref[0:1, :], gv_ref[1:2, :])
    before = lax.broadcasted_iota(jnp.int32, (tok_rows, tok_rows), 0) < lax.broadcasted_iota(
        jnp.int32, (tok_rows, tok_rows), 1
    )
    live8 = jnp.broadcast_to(live, (8, tok_rows))
    slot = dot_nn(live8.astype(BF16), jnp.where(before, 1.0, 0.0).astype(BF16))
    row8 = lax.broadcasted_iota(jnp.int32, (8, tok_rows), 0).astype(F32)
    sel = jnp.where(slot == row8, live8, 0.0)
    sel_out[...] = sel
    selx = sel.astype(BF16)
    loads[2].wait()
    for q in range(NL):
        for h in range(2):
            cols = ds(hoff[h] + q * clw, clw, 128)
            piece = dot_nn(selx, tok_ref[:, cols])[0:4].astype(BF16)
            xmsg[q, :, h * clw : (h + 1) * clw] = piece
    xrcv[pl.ds(z, 1)] = xmsg[pl.ds(r, 1)]

    for n in (4, 5, 6):
        loads[n].wait()
    pl.semaphore_wait(barrier, len(peers))

    tcps = [send(xmsg.at[(z + k) % NL], xrcv.at[z], at_z(k)) for k in zfar]

    whole = (wg, wu, wd)
    hh = hloc // 2
    wfirst, wrest = [None] * 3, [[], [], []]

    def weight_out(n):
        mine = whole[n].at[:, shard_of(dp)]
        wfirst[n] = [send(mine, mine, at_dp(at_y(k))) for k in ((1, -1) if ny > 2 else (1,))]
        wrest[n].append(send(mine, mine, partner))

    def weight_on(n):
        second = []
        for k, cp in zip((1, -1), wfirst[n]):
            cp.wait()
            cols = shard_of(at_y(-k))
            if ny > 2:
                part = whole[n].at[pl.ds(0 if k == 1 else hh, hh), cols]
                second.append(send(part, part, at_dp(at_y(k))))
            part = whole[n].at[:, cols]
            wrest[n].append(send(part, part, partner))
        return second

    def weight_end(n, second):
        wait_all(second)
        if ny > 2:
            part = whole[n].at[:, shard_of(at_y(2))]
            wrest[n].append(send(part, part, partner))

    weight_out(0)
    weight_out(1)

    loads[3].wait()
    gsel = sel * gate
    g0 = jnp.sum(gsel[0:1], axis=1, keepdims=True)
    g1 = jnp.sum(gsel[1:2], axis=1, keepdims=True)
    g2 = jnp.sum(gsel[2:3], axis=1, keepdims=True)
    rowc = lax.broadcasted_iota(jnp.int32, (8, cw), 0)
    gleft = jnp.where(rowc == 3, g0, jnp.where(rowc == 4, g2, 0.0))
    gright = jnp.where(rowc == 3, g1, 0.0)
    keep3 = rowc < CAP
    for k in range(nz):
        col = ((k % NL) * nh + k // NL) * cw
        for h, extra in ((0, gleft), (1, gright)):
            cols = ds(hoff[h] + col, cw, 128)
            piece = dot_nn(selx, tgt_ref[:, cols])
            tmsg[k, :, h * cw : (h + 1) * cw] = jnp.where(keep3, piece, extra)
    trcv[pl.ds(z, 1)] = tmsg[pl.ds(z, 1)]

    def along_l(ref_of):
        out = []
        for idx, k in enumerate((1, -1)):
            src, dst = ref_of(k, idx, 0, clw)
            out.append(send(src, dst, at_z(k)))
        for k, lo in ((2, 0), (-2, clw // 2)):
            src, dst = ref_of(k, 2, lo, clw // 2)
            out.append(send(src, dst, at_z(k)))
        return out

    far = sorted(range(1, nh), key=lambda k: -min(k, nh - k))
    xsteps = list(range(1, nx))

    def spread1(full):
        out = []
        for k in far:
            for h in range(2):
                part = full.at[xrows, ds(hoff[h] + blk * cw, cw, 128)]
                out.append(send(part, part, at_z(NL * k)))
        return out

    def spread2(full, between=()):
        def l_send(rws, h):
            def ref_of(k, idx, lo, n):
                part = full.at[rws, class_of(0, h, lo, n)]
                return part, part

            return along_l(ref_of)

        def x_send(k, h):
            part = full.at[xrows, class_of(k, h)]
            return [send(part, part, at_x(d)) for d in xsteps]

        first = l_send(xrows, 0)
        second = x_send(0, 1)
        last = x_send(0, 0) + l_send(xrows, 1)
        for q in range(3):
            if q < len(between):
                between[q]()
            if q < 2:
                first[q].wait()
            else:
                wait_all(first[2:])
            last += x_send((-1, 1, 2)[q], 0)
            if q < nx - 1:
                second[q].wait()
                last += l_send(rows_of(-xsteps[q]), 1)
        return last

    lsteps = (1, -1, 2, 0)
    xorder = xsteps + [0]

    def fold_right(n, part):
        out = []
        for q, d in enumerate(xorder):

            def ref_of(k, idx, lo, size):
                return part.at[rows_of(d), class_of(k, 1, lo, size)], rl1.at[n, q, idx, :, pl.ds(lo, size)]

            out.append(along_l(ref_of))
        return out

    def fold_left(n, part, q):
        cols = class_of(lsteps[q], 0)
        return [send(part.at[rows_of(k), cols], rx0.at[n, k - 1, q], at_x(k)) for k in xsteps]

    def fold2(n, part, left, right):
        out = []
        for q in range(NL):
            if q < nx:
                wait_all(right[q])
                total = part[rows_of(xorder[q]), class_of(0, 1)].astype(F32)
                for k in range(NL - 1):
                    total += rl1[n, q, k].astype(F32)
                s1[n, q] = total.astype(BF16)
                if xorder[q]:
                    out.append(send(s1.at[n, q], rx1.at[n, q], at_x(xorder[q])))
            wait_all(left[q])
            total = part[xrows, class_of(lsteps[q], 0)].astype(F32)
            for k in range(nx - 1):
                total += rx0[n, k, q].astype(F32)
            s0[n, q] = total.astype(BF16)
            if q < 2:
                out.append(send(s0.at[n, q], rl0.at[n, q], at_z(lsteps[q])))
            elif q == 2:
                for k, lo in ((2, 0), (-2, clw // 2)):
                    cols = pl.ds(lo, clw // 2)
                    out.append(send(s0.at[n, q, :, cols], rl0.at[n, q, :, cols], at_z(k)))
        return out

    def class_sums(n, copies):
        wait_all(copies)
        left = s0[n, NL - 1].astype(F32)
        for k in range(NL - 1):
            left += rl0[n, k].astype(F32)
        right = s1[n, nx - 1].astype(F32)
        for k in range(nx - 1):
            right += rx1[n, k].astype(F32)
        return left, right

    def fold3(n, copies):
        for h, total in enumerate(class_sums(n, copies)):
            tt[n, h] = total.astype(BF16)
        out = []
        for k in far:
            for h in range(2):
                src = tt.at[n, h, :, ds((zh + k) % nh * cw, cw, 128)]
                out.append(send(src, rh.at[n, h, k - 1], at_z(NL * k)))
        return out

    def fold4(n, copies):
        wait_all(copies)
        out = []
        for h in range(2):
            total = tt[n, h, :, ds(zh * cw, cw, 128)].astype(F32)
            for k in range(nh - 1):
                total += rh[n, h, k].astype(F32)
            out.append(total)
        return out

    seconds = [weight_on(0)]
    weight_out(2)
    wait_all(tcps)
    for k in range(nz):
        xs[CAP * k : CAP * k + 3, :] = xrcv[k].astype(F32)[0:3]
    for h in range(2):
        fx[xrows, class_of(0, h)] = xs[:, h * clw : (h + 1) * clw].astype(BF16)

    def up_then_down():
        seconds.append(weight_on(1))

    cps = spread2(
        fx,
        (up_then_down, lambda: weight_end(0, seconds[0]), lambda: seconds.append(weight_on(2))),
    )
    tcps = [send(tmsg.at[(z + k) % nz], trcv.at[z], at_z(k)) for k in zfar]
    weight_end(1, seconds[1])
    wait_all(cps)
    wait_all(wrest[0] + wrest[1])

    xc[dp] = fx[:, shard_of(dp)]
    gacc[...] = dot_nt(fx[...], wg[...])
    uacc[...] = dot_nt(fx[...], wu[...])
    pre = gacc[...]
    hid[...] = (jax.nn.sigmoid(pre) * pre * uacc[...]).astype(BF16)

    def produce_right(n, part, block):
        for k in lsteps:
            cols = class_of(k, 1)
            part[:, cols] = block(cols).astype(BF16)
        return fold_right(n, part)

    def produce_left(n, part, block):
        left = []
        for q, k in enumerate(lsteps):
            cols = class_of(k, 0)
            part[:, cols] = block(cols).astype(BF16)
            left.append(fold_left(n, part, q))
        return left

    def down(cols):
        return dot_nn(hid[...], wd[:, cols])

    wait_all(wrest[2])
    right = produce_right(0, p1, down)
    weight_end(2, seconds[2])
    wait_all(wrest[2][3 if ny > 2 else 2 :])
    left = produce_left(0, p1, down)
    xcopies = []
    for k in range(1, ndp):
        i = (dp + k) % ndp
        xcopies.append(send(fx.at[:, shard_of(i)], xc.at[dp], at_dp(i)))
    wait_all(tcps)
    for k in range(nz):
        b = CAP * k
        ts[b : b + 3, :] = trcv[k, 0:3, :]
        gs[b : b + 1, :] = trcv[k, 3:4, 0:cw]
        gs[b + 1 : b + 2, :] = trcv[k, 3:4, cw : 2 * cw]
        gs[b + 2 : b + 3, :] = trcv[k, 4:5, 0:cw]
    cps = fold2(0, p1, left, right)
    cps = fold3(0, cps)
    sums = fold4(0, cps)
    for h in range(2):
        weight = gs[...]
        residual = weight * sums[h] - ts[:, h * cw : (h + 1) * cw]
        fc[xrows, ds(hoff[h] + blk * cw, cw, 128)] = (weight * residual).astype(BF16)
    wait_all(spread1(fc))
    wait_all(spread2(fc))

    grad = dot_nt(fc[...], wd[...])
    pre = gacc[...]
    sig = jax.nn.sigmoid(pre)
    hid[...] = (grad * uacc[...] * (sig * (1.0 + pre * (1.0 - sig)))).astype(BF16)
    ua[...] = (grad * (sig * pre)).astype(BF16)
    if hp > hloc:
        gga[dp] = jnp.zeros((rall, 2 * hp), BF16)
    gga[dp, :, 0:hloc] = hid[...]
    gga[dp, :, hp : hp + hloc] = ua[...]
    gsends = [send(gga.at[dp], gga.at[dp], at_dp(at_y(k))) for k in range(1, ny)]
    gcore = [send(gga.at[dp], gga.at[dp], partner)]

    def back(cols):
        return dot_nn(hid[...], wg[:, cols]) + dot_nn(ua[...], wu[:, cols])

    right = produce_right(1, p2, back)
    left = produce_left(1, p2, back)
    cps = fold2(1, p2, left, right)
    for k, cp in enumerate(gsends, 1):
        cp.wait()
        i = at_y(-k)
        gcore.append(send(gga.at[i], gga.at[i], partner))
    rg[slots : slots + 8, :] = jnp.zeros((8, 2 * clw), F32)
    for h, total in enumerate(class_sums(1, cps)):
        rg[0:slots, h * clw : (h + 1) * clw] = total
    for k in range(nz):
        msg2[k] = rg[CAP * k : CAP * k + 8, :][0:4].astype(BF16)
    rmsg2[pl.ds(z, 1)] = msg2[pl.ds(z, 1)]
    tcps = [send(msg2.at[(z + k) % nz], rmsg2.at[z], at_z(k)) for k in zfar]
    wait_all(gcore)
    wait_all(xcopies)

    cb = min(256, dsh)
    for lo, out_ref in ((0, gg_out), (hp, ug_out)):
        for b in range(0, dsh, cb):
            lhs = gga[:, :, lo : lo + hp].reshape(ndp * rall, hp)
            rhs = xc[:, :, b : b + cb].reshape(ndp * rall, cb)
            out_ref[:, b : b + cb] = dot_tn(lhs, rhs)[0:hloc].astype(BF16)

    wait_all(tcps)
    keep = lax.broadcasted_iota(jnp.int32, (4, clw), 0) < CAP
    for q in range(NL):
        for h in range(2):
            cols = slice(h * clw, (h + 1) * clw)
            total = rmsg2[q, :, cols].astype(F32)
            for k in range(1, nh):
                total += rmsg2[q + NL * k, :, cols].astype(F32)
            total = jnp.where(keep, total, 0.0)
            rows_out[:, ds(hoff[h] + q * clw, clw, 128)] = jnp.concatenate([total, jnp.zeros_like(total)]).astype(BF16)


def finish_kernel(rows_ref, sel_ref, gg_ref, ug_ref, tg_out, gg_out, ug_out):
    tg_out[...] = dot_tn(sel_ref[...].astype(BF16), rows_ref[...]).astype(BF16)
    gg_out[...] = gg_ref[...]
    ug_out[...] = ug_ref[...]


def shards(nx, ndp, ne, tokens, expert_ids, gate_values, w_gate, w_up, w_down, target):
    tok_rows, width = tokens.shape
    hloc = w_gate.shape[1]
    nz = ne // nx
    nh = nz // NL
    slots, rall = nz * CAP, ne * CAP
    half = width // 2
    cw, dsh = half // nz, width // ndp
    clw = nh * cw
    hp = -(-hloc // 128) * 128
    vmem = pl.BlockSpec(memory_space=pltpu.VMEM)

    def buf(shape, dtype=BF16):
        return pltpu.VMEM(shape, dtype)

    scratch = [
        buf((hloc, width)), buf((hloc, width)), buf((hloc, width)),
        buf((rall, width)), buf((rall, width)), buf((rall, width)), buf((rall, width)),
        buf((ndp, rall, dsh)), buf((ndp, rall, 2 * hp)),
        buf((NL, 4, 2 * clw)), buf((nz, 4, 2 * clw)),
        buf((nz, 8, 2 * cw), F32), buf((nz, 8, 2 * cw), F32),
        buf((nz, 4, 2 * clw)), buf((nz, 4, 2 * clw)),
        buf((slots, 2 * clw), F32), buf((slots, 2 * cw), F32), buf((slots, cw), F32),
        buf((slots + 8, 2 * clw), F32),
        buf((rall, hloc), F32), buf((rall, hloc), F32), buf((rall, hloc)), buf((rall, hloc)),
        buf((2, nx - 1, NL, slots, clw)), buf((2, nx, NL - 1, slots, clw)),
        buf((2, NL - 1, slots, clw)), buf((2, nx - 1, slots, clw)),
        buf((2, 2, max(nh - 1, 1), slots, cw)),
        buf((2, NL, slots, clw)), buf((2, nx, slots, clw)), buf((2, 2, slots, clw)),
        buf((tok_rows, width)), buf((tok_rows, width)),
        buf((2, tok_rows), jnp.int32), buf((2, tok_rows), F32),
        pltpu.SemaphoreType.DMA((7,)),
        pltpu.SemaphoreType.DMA((2, 300)),
    ]
    shapes = (
        jax.ShapeDtypeStruct((hloc, dsh), BF16),
        jax.ShapeDtypeStruct((hloc, dsh), BF16),
    )
    rows, sel, gate_grad, up_grad = pl.pallas_call(
        functools.partial(layer_kernel, nx, nz, ndp),
        out_shape=(
            jax.ShapeDtypeStruct((8, width), BF16),
            jax.ShapeDtypeStruct((8, tok_rows), F32),
        ) + shapes,
        in_specs=[pl.BlockSpec(memory_space=pl.ANY)] * 7,
        out_specs=(vmem,) * 4,
        scratch_shapes=scratch,
        compiler_params=pltpu.CompilerParams(
            collective_id=1, has_side_effects=True, vmem_limit_bytes=60 << 20
        ),
        name="expert_layer",
    )(tokens, target, expert_ids.T, gate_values.T, w_gate.T, w_up.T, w_down)
    token_grad, gate_grad, up_grad = pl.pallas_call(
        finish_kernel,
        out_shape=(jax.ShapeDtypeStruct((tok_rows, width), BF16),) + shapes,
        in_specs=[vmem] * 4,
        out_specs=(vmem,) * 3,
        name="finish",
    )(rows, sel, gate_grad, up_grad)
    return token_grad, gate_grad.T, up_grad.T


def solution(mesh, nx=NX):
    placed = (
        P(("dp", "expert"), None),
        P(("dp", "expert"), None),
        P(("dp", "expert"), None),
        P("dp", "expert"),
        P("dp", "expert"),
        P("expert", "dp"),
        P(("dp", "expert"), None),
    )
    return jax.shard_map(
        functools.partial(shards, nx, mesh.shape["dp"], mesh.shape["expert"]),
        mesh=mesh,
        in_specs=placed,
        out_specs=(P(("dp", "expert"), None), P("dp", "expert"), P("dp", "expert")),
        check_vma=False,
    )
```

```python
import functools

import jax
import jax.numpy as jnp
from jax import lax
from jax.experimental import pallas as pl
from jax.experimental.pallas import tpu as pltpu
from jax.sharding import PartitionSpec as P

MESH = pl.DeviceIdType.MESH
F32, BF16 = jnp.float32, jnp.bfloat16
CAP = 3
NX = 4
NL = 4


def dot_nn(a, b):
    return jnp.dot(a, b, preferred_element_type=F32)


def dot_nt(a, b):
    return lax.dot_general(a, b, (((1,), (1,)), ((), ())), preferred_element_type=F32)


def dot_tn(a, b):
    return lax.dot_general(a, b, (((0,), (0,)), ((), ())), preferred_element_type=F32)


def ds(start, size, unit):
    return pl.ds(pl.multiple_of(start, unit), size)


def layer_kernel(
    nx, nz, ndp, tok_hbm, tgt_hbm, ids_hbm, gv_hbm, wg_ref, wu_ref, wd_ref,
    rows_out, sel_out, gg_out, ug_out,
    wg, wu, wd, fx, fc, p1, p2, xc, gga,
    xmsg, xrcv, tmsg, trcv, msg2, rmsg2, xs, ts, gs, rg,
    gacc, uacc, hid, ua,
    rx0, rl1, rl0, rx1, rh, s0, s1, tt,
    tok_ref, tgt_ref, ids_ref, gv_ref, lsems, sems,
):
    nh, ny = nz // NL, ndp // 2
    tok_rows, width = tok_ref.shape
    slots, rall = nz * CAP, nx * nz * CAP
    half = width // 2
    cw = half // nz
    clw = nh * cw
    dsh = width // ndp
    hloc = wg_ref.shape[0]
    hp = gga.shape[2] // 2
    zfar = sorted(range(1, nz), key=lambda k: -min(k, nz - k))

    dp, e = lax.axis_index("dp"), lax.axis_index("expert")
    y, c = dp // 2, dp % 2
    x, z = e // nz, e % nz
    r, zh = z % NL, z // NL
    blk = r * nh + zh
    near = y * 2 // ny
    hoff = ((1 - near) * half, near * half)

    def at_z(k):
        return (dp, x * nz + (z + k + nz) % nz)

    def at_x(k):
        return (dp, (x + k + nx) % nx * nz + z)

    def at_dp(i):
        return (i, e)

    def at_y(k):
        return (y + k + ny) % ny * 2 + c

    partner = at_dp(y * 2 + 1 - c)

    def rows_of(k):
        return ds((x + k + nx) % nx * slots, slots, 16)

    def class_of(k, h, lo=0, n=None):
        return ds(hoff[h] + (r + k + NL) % NL * clw + lo, clw if n is None else n, 128)

    xrows = rows_of(0)
    used = [0]

    def send(src, dst, dev):
        n = used[0]
        used[0] += 1
        cp = pltpu.make_async_remote_copy(
            src_ref=src, dst_ref=dst, send_sem=sems.at[0, n], recv_sem=sems.at[1, n],
            device_id=dev, device_id_type=MESH,
        )
        cp.start()
        return cp

    def wait_all(copies):
        for cp in copies:
            cp.wait()

    barrier = pltpu.get_barrier_semaphore()
    peers = [at_z(k) for k in range(1, nz)] + [at_x(k) for k in range(1, nx)]
    peers += [at_dp((dp + k) % ndp) for k in range(1, ndp)]
    for dev in peers:
        pl.semaphore_signal(barrier, inc=1, device_id=dev, device_id_type=MESH)

    def shard_of(i):
        return ds(i * dsh, dsh, 128)

    pairs = (
        (ids_hbm, ids_ref), (gv_hbm, gv_ref), (tok_hbm, tok_ref), (tgt_hbm, tgt_ref),
        (wg_ref, wg.at[:, shard_of(dp)]), (wu_ref, wu.at[:, shard_of(dp)]),
        (wd_ref, wd.at[:, shard_of(dp)]),
    )
    loads = [pltpu.make_async_copy(a, b, lsems.at[n]) for n, (a, b) in enumerate(pairs)]
    for n in (0, 1, 2, 4, 5, 6, 3):
        loads[n].start()

    loads[0].wait()
    loads[1].wait()
    computed0 = ids_ref[0:1, :] < 1
    computed = jnp.logical_or(computed0, ids_ref[1:2, :] < 1)
    live = jnp.where(computed, 1.0, 0.0).astype(F32)
    gate = jnp.where(computed0, gv_ref[0:1, :], gv_ref[1:2, :])
    before = lax.broadcasted_iota(jnp.int32, (tok_rows, tok_rows), 0) < lax.broadcasted_iota(
        jnp.int32, (tok_rows, tok_rows), 1
    )
    live8 = jnp.broadcast_to(live, (8, tok_rows))
    slot = dot_nn(live8.astype(BF16), jnp.where(before, 1.0, 0.0).astype(BF16))
    row8 = lax.broadcasted_iota(jnp.int32, (8, tok_rows), 0).astype(F32)
    sel = jnp.where(slot == row8, live8, 0.0)
    sel_out[...] = sel
    selx = sel.astype(BF16)
    loads[2].wait()
    for q in range(NL):
        for h in range(2):
            cols = ds(hoff[h] + q * clw, clw, 128)
            piece = dot_nn(selx, tok_ref[:, cols])[0:4].astype(BF16)
            xmsg[q, :, h * clw : (h + 1) * clw] = piece
    xrcv[pl.ds(z, 1)] = xmsg[pl.ds(r, 1)]

    for n in (4, 5, 6):
        loads[n].wait()
    pl.semaphore_wait(barrier, len(peers))

    tcps = [send(xmsg.at[(z + k) % NL], xrcv.at[z], at_z(k)) for k in zfar]

    whole = (wg, wu, wd)
    hh = hloc // 2
    wfirst, wrest = [None] * 3, [[], [], []]

    def weight_out(n):
        mine = whole[n].at[:, shard_of(dp)]
        wfirst[n] = [send(mine, mine, at_dp(at_y(k))) for k in ((1, -1) if ny > 2 else (1,))]
        wrest[n].append(send(mine, mine, partner))

    def weight_on(n):
        second = []
        for k, cp in zip((1, -1), wfirst[n]):
            cp.wait()
            cols = shard_of(at_y(-k))
            if ny > 2:
                part = whole[n].at[pl.ds(0 if k == 1 else hh, hh), cols]
                second.append(send(part, part, at_dp(at_y(k))))
            part = whole[n].at[:, cols]
            wrest[n].append(send(part, part, partner))
        return second

    def weight_end(n, second):
        wait_all(second)
        if ny > 2:
            part = whole[n].at[:, shard_of(at_y(2))]
            wrest[n].append(send(part, part, partner))

    weight_out(0)
    weight_out(1)

    loads[3].wait()
    gsel = sel * gate
    g0 = jnp.sum(gsel[0:1], axis=1, keepdims=True)
    g1 = jnp.sum(gsel[1:2], axis=1, keepdims=True)
    g2 = jnp.sum(gsel[2:3], axis=1, keepdims=True)
    rowc = lax.broadcasted_iota(jnp.int32, (8, cw), 0)
    gleft = jnp.where(rowc == 3, g0, jnp.where(rowc == 4, g2, 0.0))
    gright = jnp.where(rowc == 3, g1, 0.0)
    keep3 = rowc < CAP
    for k in range(nz):
        col = ((k % NL) * nh + k // NL) * cw
        for h, extra in ((0, gleft), (1, gright)):
            cols = ds(hoff[h] + col, cw, 128)
            piece = dot_nn(selx, tgt_ref[:, cols])
            tmsg[k, :, h * cw : (h + 1) * cw] = jnp.where(keep3, piece, extra)
    trcv[pl.ds(z, 1)] = tmsg[pl.ds(z, 1)]

    def along_l(ref_of):
        out = []
        for idx, k in enumerate((1, -1)):
            src, dst = ref_of(k, idx, 0, clw)
            out.append(send(src, dst, at_z(k)))
        for k, lo in ((2, 0), (-2, clw // 2)):
            src, dst = ref_of(k, 2, lo, clw // 2)
            out.append(send(src, dst, at_z(k)))
        return out

    far = sorted(range(1, nh), key=lambda k: -min(k, nh - k))
    xsteps = list(range(1, nx))

    def spread1(full):
        out = []
        for k in far:
            for h in range(2):
                part = full.at[xrows, ds(hoff[h] + blk * cw, cw, 128)]
                out.append(send(part, part, at_z(NL * k)))
        return out

    def spread2(full, between=()):
        def l_send(rws, h):
            def ref_of(k, idx, lo, n):
                part = full.at[rws, class_of(0, h, lo, n)]
                return part, part

            return along_l(ref_of)

        def x_send(k, h):
            part = full.at[xrows, class_of(k, h)]
            return [send(part, part, at_x(d)) for d in xsteps]

        first = l_send(xrows, 0)
        second = x_send(0, 1)
        last = x_send(0, 0) + l_send(xrows, 1)
        for q in range(3):
            if q < len(between):
                between[q]()
            if q < 2:
                first[q].wait()
            else:
                wait_all(first[2:])
            last += x_send((-1, 1, 2)[q], 0)
            if q < nx - 1:
                second[q].wait()
                last += l_send(rows_of(-xsteps[q]), 1)
        return last

    lsteps = (1, -1, 2, 0)
    xorder = xsteps + [0]

    def fold_right(n, part):
        out = []
        for q, d in enumerate(xorder):

            def ref_of(k, idx, lo, size):
                return part.at[rows_of(d), class_of(k, 1, lo, size)], rl1.at[n, q, idx, :, pl.ds(lo, size)]

            out.append(along_l(ref_of))
        return out

    def fold_left(n, part, q):
        cols = class_of(lsteps[q], 0)
        return [send(part.at[rows_of(k), cols], rx0.at[n, k - 1, q], at_x(k)) for k in xsteps]

    def fold2(n, part, left, right):
        out = []
        for q in range(NL):
            if q < nx:
                wait_all(right[q])
                total = part[rows_of(xorder[q]), class_of(0, 1)].astype(F32)
                for k in range(NL - 1):
                    total += rl1[n, q, k].astype(F32)
                s1[n, q] = total.astype(BF16)
                if xorder[q]:
                    out.append(send(s1.at[n, q], rx1.at[n, q], at_x(xorder[q])))
            wait_all(left[q])
            total = part[xrows, class_of(lsteps[q], 0)].astype(F32)
            for k in range(nx - 1):
                total += rx0[n, k, q].astype(F32)
            s0[n, q] = total.astype(BF16)
            if q < 2:
                out.append(send(s0.at[n, q], rl0.at[n, q], at_z(lsteps[q])))
            elif q == 2:
                for k, lo in ((2, 0), (-2, clw // 2)):
                    cols = pl.ds(lo, clw // 2)
                    out.append(send(s0.at[n, q, :, cols], rl0.at[n, q, :, cols], at_z(k)))
        return out

    def class_sums(n, copies):
        wait_all(copies)
        left = s0[n, NL - 1].astype(F32)
        for k in range(NL - 1):
            left += rl0[n, k].astype(F32)
        right = s1[n, nx - 1].astype(F32)
        for k in range(nx - 1):
            right += rx1[n, k].astype(F32)
        return left, right

    def fold3(n, copies):
        for h, total in enumerate(class_sums(n, copies)):
            tt[n, h] = total.astype(BF16)
        out = []
        for k in far:
            for h in range(2):
                src = tt.at[n, h, :, ds((zh + k) % nh * cw, cw, 128)]
                out.append(send(src, rh.at[n, h, k - 1], at_z(NL * k)))
        return out

    def fold4(n, copies):
        wait_all(copies)
        out = []
        for h in range(2):
            total = tt[n, h, :, ds(zh * cw, cw, 128)].astype(F32)
            for k in range(nh - 1):
                total += rh[n, h, k].astype(F32)
            out.append(total)
        return out

    seconds = [weight_on(0)]
    weight_out(2)
    wait_all(tcps)
    for k in range(nz):
        xs[CAP * k : CAP * k + 3, :] = xrcv[k].astype(F32)[0:3]
    for h in range(2):
        fx[xrows, class_of(0, h)] = xs[:, h * clw : (h + 1) * clw].astype(BF16)

    def up_then_down():
        seconds.append(weight_on(1))

    cps = spread2(
        fx,
        (up_then_down, lambda: weight_end(0, seconds[0]), lambda: seconds.append(weight_on(2))),
    )
    tcps = [send(tmsg.at[(z + k) % nz], trcv.at[z], at_z(k)) for k in zfar]
    weight_end(1, seconds[1])
    weight_end(2, seconds[2])
    wait_all(cps)
    wait_all(wrest[0] + wrest[1])

    xc[dp] = fx[:, shard_of(dp)]
    xcopies = []
    for k in range(1, ndp):
        i = (dp + k) % ndp
        xcopies.append(send(fx.at[:, shard_of(i)], xc.at[dp], at_dp(i)))

    gacc[...] = dot_nt(fx[...], wg[...])
    uacc[...] = dot_nt(fx[...], wu[...])
    pre = gacc[...]
    hid[...] = (jax.nn.sigmoid(pre) * pre * uacc[...]).astype(BF16)

    def produce_right(n, part, block):
        for k in lsteps:
            cols = class_of(k, 1)
            part[:, cols] = block(cols).astype(BF16)
        return fold_right(n, part)

    def produce_left(n, part, block):
        left = []
        for q, k in enumerate(lsteps):
            cols = class_of(k, 0)
            part[:, cols] = block(cols).astype(BF16)
            left.append(fold_left(n, part, q))
        return left

    def down(cols):
        return dot_nn(hid[...], wd[:, cols])

    wait_all(wrest[2])
    right = produce_right(0, p1, down)
    left = produce_left(0, p1, down)
    wait_all(tcps)
    for k in range(nz):
        b = CAP * k
        ts[b : b + 3, :] = trcv[k, 0:3, :]
        gs[b : b + 1, :] = trcv[k, 3:4, 0:cw]
        gs[b + 1 : b + 2, :] = trcv[k, 3:4, cw : 2 * cw]
        gs[b + 2 : b + 3, :] = trcv[k, 4:5, 0:cw]
    cps = fold2(0, p1, left, right)
    cps = fold3(0, cps)
    sums = fold4(0, cps)
    for h in range(2):
        weight = gs[...]
        residual = weight * sums[h] - ts[:, h * cw : (h + 1) * cw]
        fc[xrows, ds(hoff[h] + blk * cw, cw, 128)] = (weight * residual).astype(BF16)
    wait_all(spread1(fc))
    wait_all(spread2(fc))

    grad = dot_nt(fc[...], wd[...])
    pre = gacc[...]
    sig = jax.nn.sigmoid(pre)
    hid[...] = (grad * uacc[...] * (sig * (1.0 + pre * (1.0 - sig)))).astype(BF16)
    ua[...] = (grad * (sig * pre)).astype(BF16)
    if hp > hloc:
        gga[dp] = jnp.zeros((rall, 2 * hp), BF16)
    gga[dp, :, 0:hloc] = hid[...]
    gga[dp, :, hp : hp + hloc] = ua[...]
    gsends = [send(gga.at[dp], gga.at[dp], at_dp(at_y(k))) for k in range(1, ny)]
    gcore = [send(gga.at[dp], gga.at[dp], partner)]

    def back(cols):
        return dot_nn(hid[...], wg[:, cols]) + dot_nn(ua[...], wu[:, cols])

    right = produce_right(1, p2, back)
    left = produce_left(1, p2, back)
    cps = fold2(1, p2, left, right)
    for k, cp in enumerate(gsends, 1):
        cp.wait()
        i = at_y(-k)
        gcore.append(send(gga.at[i], gga.at[i], partner))
    rg[slots : slots + 8, :] = jnp.zeros((8, 2 * clw), F32)
    for h, total in enumerate(class_sums(1, cps)):
        rg[0:slots, h * clw : (h + 1) * clw] = total
    for k in range(nz):
        msg2[k] = rg[CAP * k : CAP * k + 8, :][0:4].astype(BF16)
    rmsg2[pl.ds(z, 1)] = msg2[pl.ds(z, 1)]
    tcps = [send(msg2.at[(z + k) % nz], rmsg2.at[z], at_z(k)) for k in zfar]
    wait_all(gcore)
    wait_all(xcopies)

    cb = min(256, dsh)
    for lo, out_ref in ((0, gg_out), (hp, ug_out)):
        for b in range(0, dsh, cb):
            lhs = gga[:, :, lo : lo + hp].reshape(ndp * rall, hp)
            rhs = xc[:, :, b : b + cb].reshape(ndp * rall, cb)
            out_ref[:, b : b + cb] = dot_tn(lhs, rhs)[0:hloc].astype(BF16)

    wait_all(tcps)
    keep = lax.broadcasted_iota(jnp.int32, (4, clw), 0) < CAP
    for q in range(NL):
        for h in range(2):
            cols = slice(h * clw, (h + 1) * clw)
            total = rmsg2[q, :, cols].astype(F32)
            for k in range(1, nh):
                total += rmsg2[q + NL * k, :, cols].astype(F32)
            total = jnp.where(keep, total, 0.0)
            rows_out[:, ds(hoff[h] + q * clw, clw, 128)] = jnp.concatenate([total, jnp.zeros_like(total)]).astype(BF16)


def finish_kernel(rows_ref, sel_ref, gg_ref, ug_ref, tg_out, gg_out, ug_out):
    tg_out[...] = dot_tn(sel_ref[...].astype(BF16), rows_ref[...]).astype(BF16)
    gg_out[...] = gg_ref[...]
    ug_out[...] = ug_ref[...]


def shards(nx, ndp, ne, tokens, expert_ids, gate_values, w_gate, w_up, w_down, target):
    tok_rows, width = tokens.shape
    hloc = w_gate.shape[1]
    nz = ne // nx
    nh = nz // NL
    slots, rall = nz * CAP, ne * CAP
    half = width // 2
    cw, dsh = half // nz, width // ndp
    clw = nh * cw
    hp = -(-hloc // 128) * 128
    vmem = pl.BlockSpec(memory_space=pltpu.VMEM)

    def buf(shape, dtype=BF16):
        return pltpu.VMEM(shape, dtype)

    scratch = [
        buf((hloc, width)), buf((hloc, width)), buf((hloc, width)),
        buf((rall, width)), buf((rall, width)), buf((rall, width)), buf((rall, width)),
        buf((ndp, rall, dsh)), buf((ndp, rall, 2 * hp)),
        buf((NL, 4, 2 * clw)), buf((nz, 4, 2 * clw)),
        buf((nz, 8, 2 * cw), F32), buf((nz, 8, 2 * cw), F32),
        buf((nz, 4, 2 * clw)), buf((nz, 4, 2 * clw)),
        buf((slots, 2 * clw), F32), buf((slots, 2 * cw), F32), buf((slots, cw), F32),
        buf((slots + 8, 2 * clw), F32),
        buf((rall, hloc), F32), buf((rall, hloc), F32), buf((rall, hloc)), buf((rall, hloc)),
        buf((2, nx - 1, NL, slots, clw)), buf((2, nx, NL - 1, slots, clw)),
        buf((2, NL - 1, slots, clw)), buf((2, nx - 1, slots, clw)),
        buf((2, 2, max(nh - 1, 1), slots, cw)),
        buf((2, NL, slots, clw)), buf((2, nx, slots, clw)), buf((2, 2, slots, clw)),
        buf((tok_rows, width)), buf((tok_rows, width)),
        buf((2, tok_rows), jnp.int32), buf((2, tok_rows), F32),
        pltpu.SemaphoreType.DMA((7,)),
        pltpu.SemaphoreType.DMA((2, 300)),
    ]
    shapes = (
        jax.ShapeDtypeStruct((hloc, dsh), BF16),
        jax.ShapeDtypeStruct((hloc, dsh), BF16),
    )
    rows, sel, gate_grad, up_grad = pl.pallas_call(
        functools.partial(layer_kernel, nx, nz, ndp),
        out_shape=(
            jax.ShapeDtypeStruct((8, width), BF16),
            jax.ShapeDtypeStruct((8, tok_rows), F32),
        ) + shapes,
        in_specs=[pl.BlockSpec(memory_space=pl.ANY)] * 7,
        out_specs=(vmem,) * 4,
        scratch_shapes=scratch,
        compiler_params=pltpu.CompilerParams(
            collective_id=1, has_side_effects=True, vmem_limit_bytes=60 << 20
        ),
        name="expert_layer",
    )(tokens, target, expert_ids.T, gate_values.T, w_gate.T, w_up.T, w_down)
    token_grad, gate_grad, up_grad = pl.pallas_call(
        finish_kernel,
        out_shape=(jax.ShapeDtypeStruct((tok_rows, width), BF16),) + shapes,
        in_specs=[vmem] * 4,
        out_specs=(vmem,) * 3,
        name="finish",
    )(rows, sel, gate_grad, up_grad)
    return token_grad, gate_grad.T, up_grad.T


def solution(mesh, nx=NX):
    placed = (
        P(("dp", "expert"), None),
        P(("dp", "expert"), None),
        P(("dp", "expert"), None),
        P("dp", "expert"),
        P("dp", "expert"),
        P("expert", "dp"),
        P(("dp", "expert"), None),
    )
    return jax.shard_map(
        functools.partial(shards, nx, mesh.shape["dp"], mesh.shape["expert"]),
        mesh=mesh,
        in_specs=placed,
        out_specs=(P(("dp", "expert"), None), P("dp", "expert"), P("dp", "expert")),
        check_vma=False,
    )
```

```python
import functools

import jax
import jax.numpy as jnp
from jax import lax
from jax.experimental import pallas as pl
from jax.experimental.pallas import tpu as pltpu
from jax.sharding import PartitionSpec as P

MESH = pl.DeviceIdType.MESH
F32, BF16 = jnp.float32, jnp.bfloat16
CAP = 3
NX = 4
NL = 4


def dot_nn(a, b):
    return jnp.dot(a, b, preferred_element_type=F32)


def dot_nt(a, b):
    return lax.dot_general(a, b, (((1,), (1,)), ((), ())), preferred_element_type=F32)


def dot_tn(a, b):
    return lax.dot_general(a, b, (((0,), (0,)), ((), ())), preferred_element_type=F32)


def ds(start, size, unit):
    return pl.ds(pl.multiple_of(start, unit), size)


def layer_kernel(
    nx, nz, ndp, tok_hbm, tgt_hbm, ids_hbm, gv_hbm, wg_ref, wu_ref, wd_ref,
    rows_out, sel_out, gg_out, ug_out,
    wg, wu, wd, fx, fc, p1, p2, xc, gga,
    xmsg, xrcv, tmsg, trcv, msg2, rmsg2, xs, ts, gs, rg,
    gacc, uacc, hid, ua,
    rx0, rl1, rl0, rx1, rh, s0, s1, tt,
    tok_ref, tgt_ref, ids_ref, gv_ref, lsems, sems,
):
    nh, ny = nz // NL, ndp // 2
    tok_rows, width = tok_ref.shape
    slots, rall = nz * CAP, nx * nz * CAP
    half = width // 2
    cw = half // nz
    clw = nh * cw
    dsh = width // ndp
    hloc = wg_ref.shape[0]
    hp = gga.shape[2] // 2
    zfar = sorted(range(1, nz), key=lambda k: -min(k, nz - k))

    dp, e = lax.axis_index("dp"), lax.axis_index("expert")
    y, c = dp // 2, dp % 2
    x, z = e // nz, e % nz
    r, zh = z % NL, z // NL
    blk = r * nh + zh
    near = y * 2 // ny
    hoff = ((1 - near) * half, near * half)

    def at_z(k):
        return (dp, x * nz + (z + k + nz) % nz)

    def at_x(k):
        return (dp, (x + k + nx) % nx * nz + z)

    def at_dp(i):
        return (i, e)

    def at_y(k):
        return (y + k + ny) % ny * 2 + c

    partner = at_dp(y * 2 + 1 - c)

    def rows_of(k):
        return ds((x + k + nx) % nx * slots, slots, 16)

    def class_of(k, h, lo=0, n=None):
        return ds(hoff[h] + (r + k + NL) % NL * clw + lo, clw if n is None else n, 128)

    xrows = rows_of(0)
    used = [0]

    def send(src, dst, dev):
        n = used[0]
        used[0] += 1
        cp = pltpu.make_async_remote_copy(
            src_ref=src, dst_ref=dst, send_sem=sems.at[0, n], recv_sem=sems.at[1, n],
            device_id=dev, device_id_type=MESH,
        )
        cp.start()
        return cp

    def wait_all(copies):
        for cp in copies:
            cp.wait()

    barrier = pltpu.get_barrier_semaphore()
    peers = [at_z(k) for k in range(1, nz)] + [at_x(k) for k in range(1, nx)]
    peers += [at_dp((dp + k) % ndp) for k in range(1, ndp)]
    for dev in peers:
        pl.semaphore_signal(barrier, inc=1, device_id=dev, device_id_type=MESH)

    def shard_of(i):
        return ds(i * dsh, dsh, 128)

    pairs = (
        (ids_hbm, ids_ref), (gv_hbm, gv_ref), (tok_hbm, tok_ref), (tgt_hbm, tgt_ref),
        (wg_ref, wg.at[:, shard_of(dp)]), (wu_ref, wu.at[:, shard_of(dp)]),
        (wd_ref, wd.at[:, shard_of(dp)]),
    )
    loads = [pltpu.make_async_copy(a, b, lsems.at[n]) for n, (a, b) in enumerate(pairs)]
    for n in (4, 5, 6, 0, 1, 2, 3):
        loads[n].start()
    for n in (4, 5, 6):
        loads[n].wait()
    pl.semaphore_wait(barrier, len(peers))

    whole = (wg, wu, wd)
    hh = hloc // 2
    wfirst, wrest = [None] * 3, [[], [], []]

    def weight_out(n):
        mine = whole[n].at[:, shard_of(dp)]
        wfirst[n] = [send(mine, mine, at_dp(at_y(k))) for k in ((1, -1) if ny > 2 else (1,))]
        wrest[n].append(send(mine, mine, partner))

    def weight_on(n):
        second = []
        for k, cp in zip((1, -1), wfirst[n]):
            cp.wait()
            cols = shard_of(at_y(-k))
            if ny > 2:
                part = whole[n].at[pl.ds(0 if k == 1 else hh, hh), cols]
                second.append(send(part, part, at_dp(at_y(k))))
            part = whole[n].at[:, cols]
            wrest[n].append(send(part, part, partner))
        return second

    def weight_end(n, second):
        wait_all(second)
        if ny > 2:
            part = whole[n].at[:, shard_of(at_y(2))]
            wrest[n].append(send(part, part, partner))

    weight_out(0)
    weight_out(1)

    loads[0].wait()
    loads[1].wait()
    computed0 = ids_ref[0:1, :] < 1
    computed = jnp.logical_or(computed0, ids_ref[1:2, :] < 1)
    live = jnp.where(computed, 1.0, 0.0).astype(F32)
    gate = jnp.where(computed0, gv_ref[0:1, :], gv_ref[1:2, :])
    before = lax.broadcasted_iota(jnp.int32, (tok_rows, tok_rows), 0) < lax.broadcasted_iota(
        jnp.int32, (tok_rows, tok_rows), 1
    )
    live8 = jnp.broadcast_to(live, (8, tok_rows))
    slot = dot_nn(live8.astype(BF16), jnp.where(before, 1.0, 0.0).astype(BF16))
    row8 = lax.broadcasted_iota(jnp.int32, (8, tok_rows), 0).astype(F32)
    sel = jnp.where(slot == row8, live8, 0.0)
    sel_out[...] = sel
    selx = sel.astype(BF16)
    loads[2].wait()
    for q in range(NL):
        for h in range(2):
            cols = ds(hoff[h] + q * clw, clw, 128)
            piece = dot_nn(selx, tok_ref[:, cols])[0:4].astype(BF16)
            xmsg[q, :, h * clw : (h + 1) * clw] = piece
    xrcv[pl.ds(z, 1)] = xmsg[pl.ds(r, 1)]

    tcps = [send(xmsg.at[(z + k) % NL], xrcv.at[z], at_z(k)) for k in zfar]

    loads[3].wait()
    gsel = sel * gate
    g0 = jnp.sum(gsel[0:1], axis=1, keepdims=True)
    g1 = jnp.sum(gsel[1:2], axis=1, keepdims=True)
    g2 = jnp.sum(gsel[2:3], axis=1, keepdims=True)
    rowc = lax.broadcasted_iota(jnp.int32, (8, cw), 0)
    gleft = jnp.where(rowc == 3, g0, jnp.where(rowc == 4, g2, 0.0))
    gright = jnp.where(rowc == 3, g1, 0.0)
    keep3 = rowc < CAP
    for k in range(nz):
        col = ((k % NL) * nh + k // NL) * cw
        for h, extra in ((0, gleft), (1, gright)):
            cols = ds(hoff[h] + col, cw, 128)
            piece = dot_nn(selx, tgt_ref[:, cols])
            tmsg[k, :, h * cw : (h + 1) * cw] = jnp.where(keep3, piece, extra)
    trcv[pl.ds(z, 1)] = tmsg[pl.ds(z, 1)]

    def along_l(ref_of):
        out = []
        for idx, k in enumerate((1, -1)):
            src, dst = ref_of(k, idx, 0, clw)
            out.append(send(src, dst, at_z(k)))
        for k, lo in ((2, 0), (-2, clw // 2)):
            src, dst = ref_of(k, 2, lo, clw // 2)
            out.append(send(src, dst, at_z(k)))
        return out

    far = sorted(range(1, nh), key=lambda k: -min(k, nh - k))
    xsteps = list(range(1, nx))

    def spread1(full):
        out = []
        for k in far:
            for h in range(2):
                part = full.at[xrows, ds(hoff[h] + blk * cw, cw, 128)]
                out.append(send(part, part, at_z(NL * k)))
        return out

    def spread2(full, between=()):
        def l_send(rws, h):
            def ref_of(k, idx, lo, n):
                part = full.at[rws, class_of(0, h, lo, n)]
                return part, part

            return along_l(ref_of)

        def x_send(k, h):
            part = full.at[xrows, class_of(k, h)]
            return [send(part, part, at_x(d)) for d in xsteps]

        first = l_send(xrows, 0)
        second = x_send(0, 1)
        last = x_send(0, 0) + l_send(xrows, 1)
        for q in range(3):
            if q < len(between):
                between[q]()
            if q < 2:
                first[q].wait()
            else:
                wait_all(first[2:])
            last += x_send((-1, 1, 2)[q], 0)
            if q < nx - 1:
                second[q].wait()
                last += l_send(rows_of(-xsteps[q]), 1)
        return last

    lsteps = (1, -1, 2, 0)
    xorder = xsteps + [0]

    def fold_right(n, part):
        out = []
        for q, d in enumerate(xorder):

            def ref_of(k, idx, lo, size):
                return part.at[rows_of(d), class_of(k, 1, lo, size)], rl1.at[n, q, idx, :, pl.ds(lo, size)]

            out.append(along_l(ref_of))
        return out

    def fold_left(n, part, q):
        cols = class_of(lsteps[q], 0)
        return [send(part.at[rows_of(k), cols], rx0.at[n, k - 1, q], at_x(k)) for k in xsteps]

    def fold2(n, part, left, right):
        out = []
        for q in range(NL):
            if q < nx:
                wait_all(right[q])
                total = part[rows_of(xorder[q]), class_of(0, 1)].astype(F32)
                for k in range(NL - 1):
                    total += rl1[n, q, k].astype(F32)
                s1[n, q] = total.astype(BF16)
                if xorder[q]:
                    out.append(send(s1.at[n, q], rx1.at[n, q], at_x(xorder[q])))
            wait_all(left[q])
            total = part[xrows, class_of(lsteps[q], 0)].astype(F32)
            for k in range(nx - 1):
                total += rx0[n, k, q].astype(F32)
            s0[n, q] = total.astype(BF16)
            if q < 2:
                out.append(send(s0.at[n, q], rl0.at[n, q], at_z(lsteps[q])))
            elif q == 2:
                for k, lo in ((2, 0), (-2, clw // 2)):
                    cols = pl.ds(lo, clw // 2)
                    out.append(send(s0.at[n, q, :, cols], rl0.at[n, q, :, cols], at_z(k)))
        return out

    def class_sums(n, copies):
        wait_all(copies)
        left = s0[n, NL - 1].astype(F32)
        for k in range(NL - 1):
            left += rl0[n, k].astype(F32)
        right = s1[n, nx - 1].astype(F32)
        for k in range(nx - 1):
            right += rx1[n, k].astype(F32)
        return left, right

    def fold3(n, copies):
        for h, total in enumerate(class_sums(n, copies)):
            tt[n, h] = total.astype(BF16)
        out = []
        for k in far:
            for h in range(2):
                src = tt.at[n, h, :, ds((zh + k) % nh * cw, cw, 128)]
                out.append(send(src, rh.at[n, h, k - 1], at_z(NL * k)))
        return out

    def fold4(n, copies):
        wait_all(copies)
        out = []
        for h in range(2):
            total = tt[n, h, :, ds(zh * cw, cw, 128)].astype(F32)
            for k in range(nh - 1):
                total += rh[n, h, k].astype(F32)
            out.append(total)
        return out

    seconds = [weight_on(0)]
    weight_out(2)
    wait_all(tcps)
    for k in range(nz):
        xs[CAP * k : CAP * k + 3, :] = xrcv[k].astype(F32)[0:3]
    for h in range(2):
        fx[xrows, class_of(0, h)] = xs[:, h * clw : (h + 1) * clw].astype(BF16)

    def up_then_down():
        seconds.append(weight_on(1))

    cps = spread2(
        fx,
        (up_then_down, lambda: weight_end(0, seconds[0]), lambda: seconds.append(weight_on(2))),
    )
    tcps = [send(tmsg.at[(z + k) % nz], trcv.at[z], at_z(k)) for k in zfar]
    weight_end(1, seconds[1])
    weight_end(2, seconds[2])
    wait_all(cps)
    wait_all(wrest[0] + wrest[1])

    xc[dp] = fx[:, shard_of(dp)]
    xcopies = []
    for k in range(1, ndp):
        i = (dp + k) % ndp
        xcopies.append(send(fx.at[:, shard_of(i)], xc.at[dp], at_dp(i)))

    gacc[...] = dot_nt(fx[...], wg[...])
    uacc[...] = dot_nt(fx[...], wu[...])
    pre = gacc[...]
    hid[...] = (jax.nn.sigmoid(pre) * pre * uacc[...]).astype(BF16)

    def produce_right(n, part, block):
        for k in lsteps:
            cols = class_of(k, 1)
            part[:, cols] = block(cols).astype(BF16)
        return fold_right(n, part)

    def produce_left(n, part, block):
        left = []
        for q, k in enumerate(lsteps):
            cols = class_of(k, 0)
            part[:, cols] = block(cols).astype(BF16)
            left.append(fold_left(n, part, q))
        return left

    def down(cols):
        return dot_nn(hid[...], wd[:, cols])

    wait_all(wrest[2])
    right = produce_right(0, p1, down)
    left = produce_left(0, p1, down)
    wait_all(tcps)
    for k in range(nz):
        b = CAP * k
        ts[b : b + 3, :] = trcv[k, 0:3, :]
        gs[b : b + 1, :] = trcv[k, 3:4, 0:cw]
        gs[b + 1 : b + 2, :] = trcv[k, 3:4, cw : 2 * cw]
        gs[b + 2 : b + 3, :] = trcv[k, 4:5, 0:cw]
    cps = fold2(0, p1, left, right)
    cps = fold3(0, cps)
    sums = fold4(0, cps)
    for h in range(2):
        weight = gs[...]
        residual = weight * sums[h] - ts[:, h * cw : (h + 1) * cw]
        fc[xrows, ds(hoff[h] + blk * cw, cw, 128)] = (weight * residual).astype(BF16)
    wait_all(spread1(fc))
    wait_all(spread2(fc))

    grad = dot_nt(fc[...], wd[...])
    pre = gacc[...]
    sig = jax.nn.sigmoid(pre)
    hid[...] = (grad * uacc[...] * (sig * (1.0 + pre * (1.0 - sig)))).astype(BF16)
    ua[...] = (grad * (sig * pre)).astype(BF16)
    if hp > hloc:
        gga[dp] = jnp.zeros((rall, 2 * hp), BF16)
    gga[dp, :, 0:hloc] = hid[...]
    gga[dp, :, hp : hp + hloc] = ua[...]
    gsends = [send(gga.at[dp], gga.at[dp], at_dp(at_y(k))) for k in range(1, ny)]
    gcore = [send(gga.at[dp], gga.at[dp], partner)]

    def back(cols):
        return dot_nn(hid[...], wg[:, cols]) + dot_nn(ua[...], wu[:, cols])

    right = produce_right(1, p2, back)
    left = produce_left(1, p2, back)
    cps = fold2(1, p2, left, right)
    for k, cp in enumerate(gsends, 1):
        cp.wait()
        i = at_y(-k)
        gcore.append(send(gga.at[i], gga.at[i], partner))
    rg[slots : slots + 8, :] = jnp.zeros((8, 2 * clw), F32)
    for h, total in enumerate(class_sums(1, cps)):
        rg[0:slots, h * clw : (h + 1) * clw] = total
    for k in range(nz):
        msg2[k] = rg[CAP * k : CAP * k + 8, :][0:4].astype(BF16)
    rmsg2[pl.ds(z, 1)] = msg2[pl.ds(z, 1)]
    tcps = [send(msg2.at[(z + k) % nz], rmsg2.at[z], at_z(k)) for k in zfar]
    wait_all(gcore)
    wait_all(xcopies)

    cb = min(256, dsh)
    for lo, out_ref in ((0, gg_out), (hp, ug_out)):
        for b in range(0, dsh, cb):
            lhs = gga[:, :, lo : lo + hp].reshape(ndp * rall, hp)
            rhs = xc[:, :, b : b + cb].reshape(ndp * rall, cb)
            out_ref[:, b : b + cb] = dot_tn(lhs, rhs)[0:hloc].astype(BF16)

    wait_all(tcps)
    keep = lax.broadcasted_iota(jnp.int32, (4, clw), 0) < CAP
    for q in range(NL):
        for h in range(2):
            cols = slice(h * clw, (h + 1) * clw)
            total = rmsg2[q, :, cols].astype(F32)
            for k in range(1, nh):
                total += rmsg2[q + NL * k, :, cols].astype(F32)
            total = jnp.where(keep, total, 0.0)
            rows_out[:, ds(hoff[h] + q * clw, clw, 128)] = jnp.concatenate([total, jnp.zeros_like(total)]).astype(BF16)


def finish_kernel(rows_ref, sel_ref, gg_ref, ug_ref, tg_out, gg_out, ug_out):
    tg_out[...] = dot_tn(sel_ref[...].astype(BF16), rows_ref[...]).astype(BF16)
    gg_out[...] = gg_ref[...]
    ug_out[...] = ug_ref[...]


def shards(nx, ndp, ne, tokens, expert_ids, gate_values, w_gate, w_up, w_down, target):
    tok_rows, width = tokens.shape
    hloc = w_gate.shape[1]
    nz = ne // nx
    nh = nz // NL
    slots, rall = nz * CAP, ne * CAP
    half = width // 2
    cw, dsh = half // nz, width // ndp
    clw = nh * cw
    hp = -(-hloc // 128) * 128
    vmem = pl.BlockSpec(memory_space=pltpu.VMEM)

    def buf(shape, dtype=BF16):
        return pltpu.VMEM(shape, dtype)

    scratch = [
        buf((hloc, width)), buf((hloc, width)), buf((hloc, width)),
        buf((rall, width)), buf((rall, width)), buf((rall, width)), buf((rall, width)),
        buf((ndp, rall, dsh)), buf((ndp, rall, 2 * hp)),
        buf((NL, 4, 2 * clw)), buf((nz, 4, 2 * clw)),
        buf((nz, 8, 2 * cw), F32), buf((nz, 8, 2 * cw), F32),
        buf((nz, 4, 2 * clw)), buf((nz, 4, 2 * clw)),
        buf((slots, 2 * clw), F32), buf((slots, 2 * cw), F32), buf((slots, cw), F32),
        buf((slots + 8, 2 * clw), F32),
        buf((rall, hloc), F32), buf((rall, hloc), F32), buf((rall, hloc)), buf((rall, hloc)),
        buf((2, nx - 1, NL, slots, clw)), buf((2, nx, NL - 1, slots, clw)),
        buf((2, NL - 1, slots, clw)), buf((2, nx - 1, slots, clw)),
        buf((2, 2, max(nh - 1, 1), slots, cw)),
        buf((2, NL, slots, clw)), buf((2, nx, slots, clw)), buf((2, 2, slots, clw)),
        buf((tok_rows, width)), buf((tok_rows, width)),
        buf((2, tok_rows), jnp.int32), buf((2, tok_rows), F32),
        pltpu.SemaphoreType.DMA((7,)),
        pltpu.SemaphoreType.DMA((2, 300)),
    ]
    shapes = (
        jax.ShapeDtypeStruct((hloc, dsh), BF16),
        jax.ShapeDtypeStruct((hloc, dsh), BF16),
    )
    rows, sel, gate_grad, up_grad = pl.pallas_call(
        functools.partial(layer_kernel, nx, nz, ndp),
        out_shape=(
            jax.ShapeDtypeStruct((8, width), BF16),
            jax.ShapeDtypeStruct((8, tok_rows), F32),
        ) + shapes,
        in_specs=[pl.BlockSpec(memory_space=pl.ANY)] * 7,
        out_specs=(vmem,) * 4,
        scratch_shapes=scratch,
        compiler_params=pltpu.CompilerParams(
            collective_id=1, has_side_effects=True, vmem_limit_bytes=60 << 20
        ),
        name="expert_layer",
    )(tokens, target, expert_ids.T, gate_values.T, w_gate.T, w_up.T, w_down)
    token_grad, gate_grad, up_grad = pl.pallas_call(
        finish_kernel,
        out_shape=(jax.ShapeDtypeStruct((tok_rows, width), BF16),) + shapes,
        in_specs=[vmem] * 4,
        out_specs=(vmem,) * 3,
        name="finish",
    )(rows, sel, gate_grad, up_grad)
    return token_grad, gate_grad.T, up_grad.T


def solution(mesh, nx=NX):
    placed = (
        P(("dp", "expert"), None),
        P(("dp", "expert"), None),
        P(("dp", "expert"), None),
        P("dp", "expert"),
        P("dp", "expert"),
        P("expert", "dp"),
        P(("dp", "expert"), None),
    )
    return jax.shard_map(
        functools.partial(shards, nx, mesh.shape["dp"], mesh.shape["expert"]),
        mesh=mesh,
        in_specs=placed,
        out_specs=(P(("dp", "expert"), None), P("dp", "expert"), P("dp", "expert")),
        check_vma=False,
    )
```
